256 devices in a mesh: seq: 64 (over z, x, core), head: 4 (over y).
Axes of the slice: x: 4, y: 4, z: 8, core: 2. Of those that a mesh axis runs over, the one named last changes fastest.
Arguments:
- hidden: bfloat16 [256, 2048], P('seq', 'head'), may hold values from -6 to 6
- draft_queries: bfloat16 [256, 2048], P('seq', 'head'), may hold values from -8 to 8
- draft_keys: bfloat16 [256, 2048], P('seq', 'head'), may hold values from -6 to 6
- draft_values: bfloat16 [256, 2048], P('seq', 'head'), may hold values from -6 to 6
- cache_k: bfloat16 [4, 8, 32768, 256], P(None, 'head', 'seq'), may hold values from -8 to 8
- cache_v: bfloat16 [4, 8, 32768, 256], P(None, 'head', 'seq'), may hold values from -6 to 6
- lambdas: float32 [8], P('head'), may hold values from 0.2 to 0.8
- norm_gain: float32 [256], replicated, may hold values from 0.1 to 1.9
- out_weight: bfloat16 [2048, 2048], P('head'), may hold values from -0.125 to 0.125
- lengths: int32 [4], replicated, may hold values from 8192 to 32704, as said below
- parents: int32 [4, 64], replicated, may hold values from 0 to 63, as said below
- draft_counts: int32 [4], replicated, may hold values from 32 to 64, as said below
- accepted_path: int32 [4, 64], replicated, may hold values from 0 to 63, as said below
- accepted_count: int32 [4], replicated, may hold values from 1 to 64, as said below
Outputs:
- mixed: bfloat16 [256, 2048], P('seq', 'head')
- new_cache_k: bfloat16 [4, 8, 32768, 256], P(None, 'head', 'seq')
- new_cache_v: bfloat16 [4, 8, 32768, 256], P(None, 'head', 'seq')
The draws below stay inside these ranges and needn't reach their ends.
Inputs may be any that keep to these rules, and one draw needn't show every extreme that they name: lengths[r] + 64 <= 32768; some request has exactly 32704. parents[r, 0] = 0 and parents[r, i] < i for i >= 1. `draft_counts`: some request has 64 live slots. accepted_path[r, 0] = 0; for 0 < a < accepted_count[r], accepted_path[r, a] < draft_counts[r] and its parent is accepted_path[r, a - 1]; entries from accepted_count[r] on are 0. `accepted_count`: some request accepts 64 slots.
All inputs are finite; a program needn't handle non-finite values.
Results may differ from the reference program's by a relative error of at most 0.014.
Values may be sent and summed in bfloat16 or wider, within the bound.
A program may use at most 64 MiB of HBM per device.

```python
import jax
import jax.numpy as jnp
from jax import lax

D = 2048
HEADS = 8
QK = 128
VD = 256
SINKS = 4
DMAX = 64
REQS = 4
ROWS = 256
L = 32768
WINDOW = 4096


def lengths_of(key):
    longest = L - DMAX
    shortest = L // 4
    samples = jax.random.randint(jax.random.fold_in(key, 11), (3, REQS), shortest, longest + 1)
    heavy = jnp.min(samples, axis=0)
    chosen = jax.random.randint(jax.random.fold_in(key, 12), (), 0, REQS)
    return jnp.where(jnp.arange(REQS) == chosen, longest, heavy).astype(jnp.int32)


def tree_of(key):
    chain_request = jax.random.randint(jax.random.fold_in(key, 21), (), 0, REQS)
    is_chain = jnp.arange(REQS) == chain_request
    live_counts = jax.random.randint(jax.random.fold_in(key, 22), (REQS,), DMAX // 2, DMAX + 1)
    live_counts = jnp.where(is_chain, DMAX, live_counts).astype(jnp.int32)
    slot_index = jnp.arange(DMAX, dtype=jnp.int32)
    lowest = jnp.maximum(slot_index - 6, 0)
    spread = jnp.maximum(slot_index - lowest, 1)
    random_bits = jax.random.randint(jax.random.fold_in(key, 23), (REQS, DMAX), 0, 1 << 20)
    parent_rows = lowest[None, :] + random_bits % spread[None, :]
    parent_rows = jnp.where(is_chain[:, None], jnp.maximum(slot_index - 1, 0)[None, :], parent_rows).astype(jnp.int32)
    target_bits = jax.random.randint(jax.random.fold_in(key, 24), (REQS,), 0, 1 << 20)
    target = jnp.where(is_chain, DMAX - 1, target_bits % live_counts).astype(jnp.int32)

    def walk_one(parent_row, start_node):

        def climb_up(current, unused_step):
            return (parent_row[current], current)
        ending, visited = lax.scan(climb_up, start_node, None, length=DMAX)
        steps_up = jnp.sum((visited > 0).astype(jnp.int32))
        backward = steps_up - slot_index
        path_nodes = jnp.where(backward >= 0, visited[jnp.clip(backward, 0, DMAX - 1)], 0)
        return (path_nodes.astype(jnp.int32), (steps_up + 1).astype(jnp.int32))
    path_rows, path_lengths = jax.vmap(walk_one)(parent_rows, target)
    return (parent_rows, live_counts, path_rows, path_lengths)


def draw_lengths(key, part):
    return lengths_of(key)


def draw_parents(key, part):
    return tree_of(key)[0]


def draw_draft_counts(key, part):
    return tree_of(key)[1]


def draw_accepted_path(key, part):
    return tree_of(key)[2]


def draw_accepted_count(key, part):
    return tree_of(key)[3]


def draw_draft_queries(key, part):
    normals = jnp.clip(jax.random.normal(jax.random.fold_in(key, 41), (ROWS, HEADS * 2 * QK), jnp.float32), -6.0, 6.0)
    return normals.astype(jnp.bfloat16)


def draw_cache_k(key, part):
    normals = jnp.clip(jax.random.normal(jax.random.fold_in(key, 42), (REQS, HEADS, L, 2 * QK), jnp.float32), -6.0, 6.0)
    return normals.astype(jnp.bfloat16)


def block_scale(key, dims, cuts, smallest, high):
    factor_of = 1.0
    for dim, shards_of in cuts:
        steps = jax.random.uniform(jax.random.fold_in(jax.random.fold_in(key, 6), dim), (shards_of,), jnp.float32, smallest / len(cuts), high / len(cuts))
        factor_of = factor_of * jnp.repeat(jnp.exp(steps), dims[dim] // shards_of).reshape((-1,) + (1,) * (len(dims) - 1 - dim))
    return factor_of


def bell_draw(rng, shape, deviation, bound, cuts=(), kind=jnp.bfloat16):
    level = block_scale(rng, shape, cuts, -0.22, 0.18) if cuts else 1.0
    values = jax.random.normal(rng, shape, jnp.float32) * deviation * level
    return jnp.minimum(jnp.maximum(values, -bound), bound).astype(kind)


def setup_inputs(seed: int = 0) -> dict:
    keys = jax.random.split(jax.random.key(seed), 15)
    hidden = bell_draw(keys[0], (ROWS, D), 1.0, 6.0, ((0, 64), (1, 4)))
    draft_queries = draw_draft_queries(jax.random.fold_in(keys[14], 71), 0)
    draft_keys = bell_draw(keys[2], (ROWS, HEADS * 2 * QK), 1.0, 6.0, ((0, 64), (1, 4)))
    draft_values = bell_draw(keys[3], (ROWS, HEADS * VD), 1.0, 6.0, ((0, 64), (1, 4)))
    cache_k = draw_cache_k(jax.random.fold_in(keys[14], 71), 0)
    cache_v = bell_draw(keys[5], (REQS, HEADS, L, VD), 1.0, 6.0, ((1, 4), (2, 64)))
    lambdas = jnp.clip(0.2 + 0.6 * jax.random.uniform(keys[6], (HEADS,), jnp.float32) ** block_scale(keys[6], (HEADS,), ((0, 4),), -0.2, 0.2), 0.2, 0.8)
    norm_gain = jnp.clip(1.0 + 0.18 * jax.random.normal(keys[7], (VD,), jnp.float32), 0.1, 1.9)
    out_weight = bell_draw(keys[8], (HEADS * VD, D), (HEADS * VD) ** -0.5, 0.125, ((0, 4),))
    lengths = draw_lengths(jax.random.fold_in(keys[14], 71), 0)
    parents = draw_parents(jax.random.fold_in(keys[14], 71), 0)
    draft_counts = draw_draft_counts(jax.random.fold_in(keys[14], 71), 0)
    accepted_path = draw_accepted_path(jax.random.fold_in(keys[14], 71), 0)
    accepted_count = draw_accepted_count(jax.random.fold_in(keys[14], 71), 0)
    return {"hidden": hidden, "draft_queries": draft_queries, "draft_keys": draft_keys, "draft_values": draft_values, "cache_k": cache_k, "cache_v": cache_v, "lambdas": lambdas, "norm_gain": norm_gain, "out_weight": out_weight, "lengths": lengths, "parents": parents, "draft_counts": draft_counts, "accepted_path": accepted_path, "accepted_count": accepted_count}


FILL_LOW = -1e+30
EPSILON = 1e-05
OUT_SCALE = 0.8

def ancestors(parents):
    slot_count = parents.shape[1]
    slot_index = jnp.arange(slot_count, dtype=jnp.int32)
    parent_link = (parents[:, :, None] == slot_index[None, None, :]) & (slot_index[None, :, None] >= 1)
    ancestry = jnp.minimum(jnp.eye(slot_count, dtype=jnp.float32)[None] + parent_link.astype(jnp.float32), 1.0)
    for doubling in range(max(1, (slot_count - 1).bit_length())):
        ancestry = jnp.minimum(jnp.einsum('rij,rjk->rik', ancestry, ancestry, precision=lax.Precision.HIGHEST), 1.0)
    return ancestry

def reference(hidden, draft_queries, draft_keys, draft_values, cache_k, cache_v, lambdas, norm_gain, out_weight, lengths, parents, draft_counts, accepted_path, accepted_count):
    ancestry = ancestors(parents)
    tree_depth = (lax.optimization_barrier(jnp.sum(ancestry, axis=-1)) - 1.0).astype(jnp.int32)
    score_scale = QK ** (-0.5)
    slot_index = jnp.arange(DMAX, dtype=jnp.int32)
    position = jnp.arange(L, dtype=jnp.int32)
    query_all = draft_queries.reshape(REQS, DMAX, HEADS, 2, QK)
    key_all = draft_keys.reshape(REQS, DMAX, HEADS, 2, QK)
    value_all = draft_values.reshape(REQS, DMAX, HEADS, VD)
    cache_split = cache_k.reshape(REQS, HEADS, L, 2, QK)

    def attend(pieces):
        request_queries, request_keys, request_values, request_ck, request_cv, length, request_tree, request_depth, count_live = pieces
        query_pos = length + request_depth
        cache_mask = (position[None, :] < length) & ((position[None, :] < SINKS) | (position[None, :] > query_pos[:, None] - WINDOW))
        draft_mask = (request_tree > 0.5) & (slot_index[None, :] < count_live)
        query_wide = request_queries.astype(jnp.float32)
        cache_scores = jnp.einsum('ihmd,hpmd->ihmp', query_wide, request_ck.astype(jnp.float32)) * score_scale
        draft_scores = jnp.einsum('ihmd,jhmd->ihmj', query_wide, request_keys.astype(jnp.float32)) * score_scale
        cache_wide = cache_mask[:, None, None, :]
        draft_wide = draft_mask[:, None, None, :]
        cache_scores = jnp.where(cache_wide, cache_scores, FILL_LOW)
        draft_scores = jnp.where(draft_wide, draft_scores, FILL_LOW)
        row_peak = jnp.maximum(lax.optimization_barrier(jnp.max(cache_scores, axis=-1)), lax.optimization_barrier(jnp.max(draft_scores, axis=-1)))
        cache_weight = jnp.where(cache_wide, jnp.exp(cache_scores - row_peak[..., None]), 0.0)
        draft_weight = jnp.where(draft_wide, jnp.exp(draft_scores - row_peak[..., None]), 0.0)
        row_total = lax.optimization_barrier(jnp.sum(cache_weight, axis=-1)) + lax.optimization_barrier(jnp.sum(draft_weight, axis=-1))
        cache_round = lax.optimization_barrier(cache_weight.astype(jnp.bfloat16)).astype(jnp.float32)
        draft_round = lax.optimization_barrier(draft_weight.astype(jnp.bfloat16)).astype(jnp.float32)
        weighted = jnp.einsum('ihmp,hpv->ihmv', cache_round, request_cv.astype(jnp.float32))
        weighted = weighted + jnp.einsum('ihmj,jhv->ihmv', draft_round, request_values.astype(jnp.float32))
        return weighted / row_total[..., None]
    attended = lax.map(attend, (query_all, key_all, value_all, cache_split, cache_v, lengths, ancestry, tree_depth, draft_counts))
    mixing = lambdas.astype(jnp.float32)[None, None, :, None]
    difference = attended[:, :, :, 0] - mixing * attended[:, :, :, 1]
    mean_square = lax.optimization_barrier(jnp.mean(difference * difference, axis=-1, keepdims=True))
    normed = difference * lax.rsqrt(mean_square + EPSILON) * norm_gain * OUT_SCALE
    live_rows = slot_index[None, :] < draft_counts[:, None]
    normed = jnp.where(live_rows[:, :, None, None], normed, 0.0).astype(jnp.bfloat16).reshape(ROWS, HEADS * VD)
    mixed = (jnp.dot(normed, out_weight, preferred_element_type=jnp.float32) + hidden.astype(jnp.float32)).astype(jnp.bfloat16)
    node_rows = (accepted_path + jnp.arange(REQS, dtype=jnp.int32)[:, None] * DMAX).reshape(-1)
    kept_keys = draft_keys[node_rows].reshape(REQS, DMAX, HEADS, 2 * QK).transpose(0, 2, 1, 3)
    kept_values = draft_values[node_rows].reshape(REQS, DMAX, HEADS, VD).transpose(0, 2, 1, 3)

    def write(cache_rows, kept_rows, length, kept_total):
        existing = lax.dynamic_slice_in_dim(cache_rows, length, DMAX, axis=1)
        written = jnp.where((slot_index < kept_total)[None, :, None], kept_rows, existing)
        return lax.dynamic_update_slice_in_dim(cache_rows, written, length, axis=1)
    new_cache_k = jax.vmap(write)(cache_k, kept_keys, lengths, accepted_count)
    new_cache_v = jax.vmap(write)(cache_v, kept_values, lengths, accepted_count)
    return (mixed, new_cache_k, new_cache_v)
```

```python
import functools
import math

import jax
import jax.numpy as jnp
from jax import lax
from jax.experimental import pallas as pl
from jax.experimental.pallas import tpu as pltpu
from jax.sharding import PartitionSpec as P

MESH = pl.DeviceIdType.MESH
F32 = jnp.float32
BF16 = jnp.bfloat16
I32 = jnp.int32

SINKS = 4
FILL_LOW = -1e30
EPSILON = 1e-05
OUT_SCALE = 0.8
LOG2E = 1.4426950408889634

NC = 2
ROWS_DEV = 4
CHUNKS = 4
TILE = ROWS_DEV * CHUNKS
QK = 128
VD = 256
MSG = VD + 128


def nt(a, b):
    return lax.dot_general(a, b, (((1,), (1,)), ((), ())), preferred_element_type=F32)


def iota(shape, dim):
    return lax.broadcasted_iota(I32, shape, dim)


def slot_of(index, nx):
    row = index % ROWS_DEV
    zl = (index // TILE) % 2
    x = (index // (2 * TILE)) % nx
    core = index // (2 * TILE * nx)
    return ((zl * nx + x) * NC + core) * ROWS_DEV + row


def chunk_of(index):
    return (index // ROWS_DEV) % CHUNKS


def tile_of(ref):
    value = ref[...].astype(F32)
    pieces = [value[:, QK * c : QK * (c + 1)] for c in range(CHUNKS)]
    return jnp.concatenate(pieces, axis=0).astype(BF16)


def unpack(message):
    wide = message.astype(F32)
    shift = wide[:, VD : VD + 1]
    total = wide[:, VD + 1 : VD + 2] + wide[:, VD + 2 : VD + 3]
    return shift, total, wide[:, :VD]


def merge(parts):
    peak = functools.reduce(jnp.maximum, [p[0] for p in parts])
    factors = [jnp.exp2(p[0] - peak) for p in parts]
    total = sum(f * p[1] for f, p in zip(factors, parts))
    weighted = sum(f * p[2] for f, p in zip(factors, parts))
    return peak, total, weighted


def pack(part):
    shift, total, weighted = part
    rows = weighted.shape[0]
    high = total.astype(BF16).astype(F32)
    lane = iota((rows, 128), 1)
    stats = jnp.where(lane == 0, shift, jnp.where(lane == 1, high, total - high))
    return weighted.astype(BF16), stats.astype(BF16)


def attention_kernel(
    nz, nx, nh, window,
    lengths, draft_counts, lambdas, hidden, queries, keys, values, gain, parents, cache_k, cache_v, out_weight,
    mixed, kv_out,
    gq, gkv, kc, vc, wv, tree, part, core_in, chip, x_in, plane, z_in, y_out, y_in,
    qz_s, qz_r, qx_s, qx_r, qc_s, qc_r, kz_s, kz_r, kx_s, kx_r, kc_s, kc_r,
    rc_s, rc_r, rx_s, rx_r, rz_s, rz_r, y_s, y_r, load_sem, w_sem, out_sem,
):
    nr = nz // 2
    slots = 2 * nx * NC * ROWS_DEV
    span = cache_k.shape[2]
    rows = 2 * nx * NC * TILE
    seq = lax.axis_index("seq")
    head = lax.axis_index("head")
    core = seq % NC
    x = (seq // NC) % nx
    z = seq // (NC * nx)

    def device(zz, xx, cc):
        return ((zz * nx + xx) * NC + cc, head)

    def remote(src, dst, send, recv, target):
        return pltpu.make_async_remote_copy(
            src_ref=src, dst_ref=dst, send_sem=send, recv_sem=recv, device_id=target, device_id_type=MESH
        )

    z_peers = [(d, (z + d) % nz, (z + nz - d) % nz) for d in range(1, nz)]
    x_peers = [(d, (x + d) % nx, (x + nx - d) % nx) for d in range(1, nx)]
    h_peers = [(d, (head + d) % nh, (head + nh - d) % nh) for d in range(1, nh)]
    other = 1 - core

    barrier = pltpu.get_barrier_semaphore()
    peers = [device(z, x, other)]
    peers += [device(to, x, core) for _, to, _ in z_peers]
    peers += [device(z, to, core) for _, to, _ in x_peers]
    peers += [(seq, to) for _, to, _ in h_peers]
    for peer in peers:
        pl.semaphore_signal(barrier, inc=1, device_id=peer, device_id_type=MESH)

    loads = []
    for r in range(nr):
        loads.append(
            (
                pltpu.make_async_copy(cache_k.at[r], kc.at[r], load_sem.at[r, 0]),
                pltpu.make_async_copy(cache_v.at[r], vc.at[r], load_sem.at[r, 1]),
            )
        )
    for copy_k, copy_v in loads:
        copy_k.start()
        copy_v.start()
    load_w = pltpu.make_async_copy(out_weight, wv, w_sem)
    load_w.start()

    gq[core, x, z] = tile_of(queries)
    gkv[core, x, z, 0] = tile_of(keys)
    gkv[core, x, z, 1] = tile_of(values)

    pl.semaphore_wait(barrier, len(peers))

    sent = []

    def gather_z(buf, send, recv):
        waits = []
        for d, to, source in z_peers:
            copy = remote(buf.at[core, x, z], buf.at[core, x, z], send.at[d], recv.at[d], device(to, x, core))
            copy.start()
            sent.append(copy)
            waits.append(remote(buf.at[core, x, z], buf.at[core, x, source], send.at[d], recv.at[d], device(to, x, core)))
        return waits

    def gather_x(buf, send, recv):
        waits = []
        for d, to, source in x_peers:
            copy = remote(buf.at[core, x], buf.at[core, x], send.at[d], recv.at[d], device(z, to, core))
            copy.start()
            sent.append(copy)
            waits.append(remote(buf.at[core, x], buf.at[core, source], send.at[d], recv.at[d], device(z, to, core)))
        return waits

    def gather_core(buf, send, recv):
        copy = remote(buf.at[core], buf.at[core], send, recv, device(z, x, other))
        copy.start()
        sent.append(copy)
        return [remote(buf.at[core], buf.at[other], send, recv, device(z, x, other))]

    def arrived(waits):
        for copy in waits:
            copy.wait_recv()

    q_z = gather_z(gq, qz_s, qz_r)
    kv_z = gather_z(gkv, kz_s, kz_r)

    row_slot = slot_of(iota((rows, slots), 0), nx)
    row_pick = (row_slot == iota((rows, slots), 1)).astype(BF16)
    chunk = chunk_of(iota((rows, 1), 0))
    low = iota((slots, slots), 0)
    high = iota((slots, slots), 1)
    trees = []
    for r in range(nr):
        link = (low == parents[r : r + 1, :]) & (high >= 1)
        trees.append((link | (low == high)).astype(F32).astype(BF16))
    for _ in range(max(1, (slots - 1).bit_length())):
        trees = [jnp.minimum(jnp.dot(t, t, preferred_element_type=F32), 1.0).astype(BF16) for t in trees]
    oldest = []
    for r in range(nr):
        tree[r] = trees[r]
        depth = jnp.sum(nt(row_pick, trees[r]), axis=1, keepdims=True) - 1.0
        oldest.append(depth + (lengths[r] - window).astype(F32))

    arrived(q_z)
    q_x = gather_x(gq, qx_s, qx_r)
    arrived(q_x)
    q_c = gather_core(gq, qc_s, qc_r)
    arrived(kv_z)
    kv_x = gather_x(gkv, kx_s, kx_r)
    arrived(q_c)

    scale = LOG2E / math.sqrt(QK)
    position = (seq * span + iota((1, span), 1)).astype(F32)

    def attend(r):
        loads[r][0].wait()
        loads[r][1].wait()
        q = gq[:, :, 2 * r : 2 * r + 2].reshape(rows, QK)
        zero = jnp.zeros_like(q)
        split = [jnp.where(chunk == c, q, zero) for c in range(CHUNKS)]
        scores = nt(jnp.concatenate(split[:2], axis=1), kc[r, 0]) + nt(jnp.concatenate(split[2:], axis=1), kc[r, 1])
        reach = jnp.where(position < SINKS, -FILL_LOW, position)
        reach = jnp.where(position < lengths[r].astype(F32), reach, FILL_LOW)
        allowed = reach > oldest[r]
        scores = jnp.where(allowed, scores * scale, FILL_LOW)
        shift = jnp.max(scores, axis=1, keepdims=True).astype(BF16).astype(F32)
        weight = jnp.where(allowed, jnp.exp2(scores - shift), 0.0)
        total = jnp.sum(weight, axis=1, keepdims=True)
        weight = weight.astype(BF16)
        weighted = jnp.where(
            chunk < 2,
            jnp.dot(weight, vc[r, 0], preferred_element_type=F32),
            jnp.dot(weight, vc[r, 1], preferred_element_type=F32),
        )
        body, stats = pack((shift, total, weighted))
        part[r, :, :, :, :, :VD] = body.reshape(NC, nx, 2, TILE, VD)
        part[r, :, :, :, :, VD:] = stats.reshape(NC, nx, 2, TILE, 128)
        copy = remote(part.at[r, other], core_in.at[r], rc_s.at[r], rc_r.at[r], device(z, x, other))
        copy.start()
        sent.append(copy)
        return copy

    def chip_merge(r, copy):
        copy.wait_recv()
        block = nx * 2 * TILE
        mine = part[r, core].reshape(block, MSG)
        theirs = core_in[r].reshape(block, MSG)
        body, stats = pack(merge([unpack(mine), unpack(theirs)]))
        chip[r, :, :, :, :VD] = body.reshape(nx, 2, TILE, VD)
        chip[r, :, :, :, VD:] = stats.reshape(nx, 2, TILE, 128)
        waits = []
        for d, to, source in x_peers:
            copy = remote(chip.at[r, to], x_in.at[r, d], rx_s.at[r, d], rx_r.at[r, d], device(z, to, core))
            copy.start()
            sent.append(copy)
            waits.append(copy)
        return waits

    def plane_merge(r, waits):
        arrived(waits)
        parts = [unpack(chip[r, x].reshape(2 * TILE, MSG))]
        for d, _, _ in x_peers:
            parts.append(unpack(x_in[r, d].reshape(2 * TILE, MSG)))
        body, stats = pack(merge(parts))
        plane[r, :, :, :VD] = body.reshape(2, TILE, VD)
        plane[r, :, :, VD:] = stats.reshape(2, TILE, 128)
        for zl in range(2):
            to = 2 * r + zl

            @pl.when(z != to)
            def _():
                remote(plane.at[r, zl], z_in.at[z], rz_s.at[to], rz_r.at[z], device(to, x, core)).start()

            @pl.when(z == to)
            def _():
                z_in[z] = plane[r, zl]

    in_core = {}
    in_x = {}
    in_core[0] = attend(0)
    arrived(kv_x)
    kv_c = gather_core(gkv, kc_s, kc_r)
    for r in range(1, nr + 2):
        if r < nr:
            in_core[r] = attend(r)
        if r - 1 < nr:
            in_x[r - 1] = chip_merge(r - 1, in_core[r - 1])
        if r >= 2:
            plane_merge(r - 2, in_x[r - 2])

    arrived(kv_c)
    kv_copy = pltpu.make_async_copy(gkv, kv_out, out_sem)
    kv_copy.start()

    own = z // 2
    own_slot = ((z % 2) * nx + x) * NC + core
    own_slot = own_slot * ROWS_DEV
    keys_own = gkv[:, :, pl.ds(2 * own, 2), 0].reshape(rows, QK)
    values_own = gkv[:, :, pl.ds(2 * own, 2), 1].reshape(rows, QK)
    pick_row = (own_slot + iota((TILE, slots), 0) % ROWS_DEV == iota((TILE, slots), 1)).astype(BF16)
    live = (iota((TILE, slots), 1) < draft_counts[own]).astype(F32)
    seen = (nt(pick_row, tree[own]) * live).astype(BF16)
    pick_lane = (slot_of(iota((slots, rows), 1), nx) == iota((slots, rows), 0)).astype(BF16)
    lane_chunk = chunk_of(iota((TILE, rows), 1))
    row_chunk = iota((TILE, rows), 0) // ROWS_DEV
    allowed = (jnp.dot(seen, pick_lane, preferred_element_type=F32) > 0.5) & (lane_chunk == row_chunk)
    scores = jnp.where(allowed, nt(gq[core, x, z], keys_own) * scale, FILL_LOW)
    shift = jnp.max(scores, axis=1, keepdims=True)
    weight = jnp.where(allowed, jnp.exp2(scores - shift), 0.0)
    total = jnp.sum(weight, axis=1, keepdims=True)
    first_map = row_chunk % 2 == 0
    ahead = pltpu.roll(weight, ROWS_DEV, 1)
    behind = pltpu.roll(weight, rows - ROWS_DEV, 1)
    left = jnp.where(first_map, weight, behind).astype(BF16)
    right = jnp.where(first_map, ahead, weight).astype(BF16)
    weighted = jnp.concatenate(
        [
            jnp.dot(left, values_own, preferred_element_type=F32),
            jnp.dot(right, values_own, preferred_element_type=F32),
        ],
        axis=1,
    )
    draft = (shift, total, weighted)

    for d, to, source in z_peers:
        remote(plane.at[0, 0], z_in.at[source], rz_s.at[to], rz_r.at[source], device(to, x, core)).wait_recv()
    peak, total, weighted = merge([unpack(z_in[i]) for i in range(nz)] + [draft])
    attended = weighted / total
    row_live = own_slot + iota((ROWS_DEV, 1), 0) < draft_counts[own]
    normed = []
    for h in range(2):
        first = attended[2 * h * ROWS_DEV : (2 * h + 1) * ROWS_DEV]
        second = attended[(2 * h + 1) * ROWS_DEV : (2 * h + 2) * ROWS_DEV]
        difference = first - lambdas[h] * second
        square = jnp.mean(difference * difference, axis=1, keepdims=True)
        scaled = difference * lax.rsqrt(square + EPSILON) * gain[...] * OUT_SCALE
        normed.append(jnp.where(row_live, scaled, 0.0).astype(BF16))
    load_w.wait()
    product = jnp.dot(jnp.concatenate(normed, axis=1), wv[...], preferred_element_type=F32)
    width = mixed.shape[1]
    for h in range(nh):
        y_out[h] = product[:, h * width : (h + 1) * width]
    waits = []
    for d, to, source in h_peers:
        copy = remote(y_out.at[to], y_in.at[d], y_s.at[d], y_r.at[d], (seq, to))
        copy.start()
        sent.append(copy)
        waits.append(copy)
    summed = y_out[head]
    arrived(waits)
    for d, _, _ in h_peers:
        summed = summed + y_in[d]
    mixed[...] = (summed + hidden[...].astype(F32)).astype(BF16)

    for copy in sent:
        copy.wait_send()
    for d, to, source in z_peers:
        remote(plane.at[0, 0], z_in.at[source], rz_s.at[to], rz_r.at[source], device(to, x, core)).wait_send()
    kv_copy.wait()


def cache_kernel(
    nz, nx, lengths, accepted_count, path, mixed_in, kv, cache_k, cache_v, mixed, new_k, new_v, kvb, kb, vb, in_sem, out_sem, kv_sem
):
    nr = nz // 2
    slots = 2 * nx * NC * ROWS_DEV
    rows = 2 * nx * NC * TILE
    span = cache_k.shape[2]
    seq = lax.axis_index("seq")
    load_kv = pltpu.make_async_copy(kv, kvb, kv_sem)
    load_kv.start()
    pairs = ((cache_k, kb, new_k), (cache_v, vb, new_v))
    loads, stores = [], []
    for r in range(nr):
        loads.append([pltpu.make_async_copy(src.at[r], buf.at[r], in_sem.at[r, i]) for i, (src, buf, _) in enumerate(pairs)])
        stores.append([pltpu.make_async_copy(buf.at[r], dst.at[r], out_sem.at[r, i]) for i, (_, buf, dst) in enumerate(pairs)])
    for r in range(nr):
        for copy in loads[r]:
            copy.start()
    mixed[...] = mixed_in[...]
    reach = slots + 16
    load_kv.wait()
    for r in range(nr):
        for copy in loads[r]:
            copy.wait()
        begin = lengths[r] - seq * span
        count = accepted_count[r]

        @pl.when((begin < span) & (begin + count > 0))
        def _():
            base = jnp.clip(begin // 16 * 16, 0, span - reach)
            base = pl.multiple_of(base, 16)
            place = iota((reach, slots), 0) + (base - begin)
            order = iota((reach, slots), 1)
            taken = ((place == order) & (order < count)).astype(BF16)
            source = (path[r : r + 1, :] == iota((slots, slots), 0)).astype(BF16)
            pick = nt(taken, source).astype(BF16)
            lanes = (slot_of(iota((slots, rows), 1), nx) == iota((slots, rows), 0)).astype(BF16)
            wide = jnp.dot(pick, lanes, preferred_element_type=F32)
            lane_chunk = chunk_of(iota((reach, rows), 1))
            row_place = iota((reach, 1), 0) + (base - begin)
            touched = (row_place >= 0) & (row_place < count)
            for i, (_, buf, _) in enumerate(pairs):
                block = kvb[:, :, 2 * r : 2 * r + 2, i].reshape(rows, 128)
                for c in range(CHUNKS):
                    chosen = jnp.where(lane_chunk == c, wide, 0.0).astype(BF16)
                    fresh = jnp.dot(chosen, block, preferred_element_type=F32)
                    where = (r, c // 2, pl.ds(base, reach), pl.ds(128 * (c % 2), 128))
                    old = buf[where].astype(F32)
                    buf[where] = jnp.where(touched, fresh, old).astype(BF16)

        for copy in stores[r]:
            copy.start()
    for r in range(nr):
        for copy in stores[r]:
            copy.wait()


def body(
    nz, nx, nh, window,
    hidden, draft_queries, draft_keys, draft_values, cache_k, cache_v, lambdas, norm_gain, out_weight,
    lengths, parents, draft_counts, accepted_path, accepted_count,
):
    nr = nz // 2
    slots = 2 * nx * NC * ROWS_DEV
    vmem = pl.BlockSpec(memory_space=pltpu.VMEM)
    smem = pl.BlockSpec(memory_space=pltpu.SMEM)
    hbm = pl.BlockSpec(memory_space=pl.ANY)
    dma = pltpu.SemaphoreType.DMA
    kv_shape = (NC, nx, nz, 2, TILE, 128)
    mixed, kv = pl.pallas_call(
        functools.partial(attention_kernel, nz, nx, nh, window),
        out_shape=(jax.ShapeDtypeStruct(hidden.shape, BF16), jax.ShapeDtypeStruct(kv_shape, BF16)),
        in_specs=[smem] * 3 + [vmem] * 6 + [hbm] * 3,
        out_specs=(vmem, hbm),
        scratch_shapes=[
            pltpu.VMEM((NC, nx, nz, TILE, 128), BF16),
            pltpu.VMEM(kv_shape, BF16),
            pltpu.VMEM(cache_k.shape, BF16),
            pltpu.VMEM(cache_v.shape, BF16),
            pltpu.VMEM(out_weight.shape, BF16),
            pltpu.VMEM((nr, slots, slots), BF16),
            pltpu.VMEM((nr, NC, nx, 2, TILE, MSG), BF16),
            pltpu.VMEM((nr, nx, 2, TILE, MSG), BF16),
            pltpu.VMEM((nr, nx, 2, TILE, MSG), BF16),
            pltpu.VMEM((nr, nx, 2, TILE, MSG), BF16),
            pltpu.VMEM((nr, 2, TILE, MSG), BF16),
            pltpu.VMEM((nz, TILE, MSG), BF16),
            pltpu.VMEM((nh, ROWS_DEV, hidden.shape[1]), F32),
            pltpu.VMEM((nh, ROWS_DEV, hidden.shape[1]), F32),
            dma((nz,)), dma((nz,)), dma((nx,)), dma((nx,)), dma, dma,
            dma((nz,)), dma((nz,)), dma((nx,)), dma((nx,)), dma, dma,
            dma((nr,)), dma((nr,)), dma((nr, nx)), dma((nr, nx)), dma((nz,)), dma((nz,)), dma((nh,)), dma((nh,)),
            dma((nr, 2)), dma, dma,
        ],
        compiler_params=pltpu.CompilerParams(collective_id=0, has_side_effects=True, vmem_limit_bytes=40 << 20),
    )(
        lengths, draft_counts, lambdas, hidden, draft_queries, draft_keys, draft_values,
        norm_gain.reshape(1, VD), parents, cache_k, cache_v, out_weight,
    )
    return pl.pallas_call(
        functools.partial(cache_kernel, nz, nx),
        out_shape=(
            jax.ShapeDtypeStruct(hidden.shape, BF16),
            jax.ShapeDtypeStruct(cache_k.shape, BF16),
            jax.ShapeDtypeStruct(cache_v.shape, BF16),
        ),
        in_specs=[smem, smem, vmem, vmem, hbm, hbm, hbm],
        out_specs=(vmem, hbm, hbm),
        scratch_shapes=[
            pltpu.VMEM(kv_shape, BF16),
            pltpu.VMEM(cache_k.shape, BF16),
            pltpu.VMEM(cache_v.shape, BF16),
            dma((nr, 2)), dma((nr, 2)), dma,
        ],
        compiler_params=pltpu.CompilerParams(vmem_limit_bytes=24 << 20),
    )(lengths, accepted_count, accepted_path, mixed, kv, cache_k, cache_v)


def build(mesh, nz, nx, window):
    seq_rows = P("seq", "head")
    cache = P(None, "head", "seq", None)
    in_specs = (seq_rows,) * 4 + (cache, cache, P("head"), P(), P("head", None)) + (P(),) * 5
    return jax.shard_map(
        functools.partial(body, nz, nx, mesh.shape["head"], window),
        mesh=mesh,
        in_specs=in_specs,
        out_specs=(seq_rows, cache, cache),
        check_vma=False,
    )


def solution(mesh):
    return build(mesh, 8, 4, 4096)
```

```python
import functools
import math

import jax
import jax.numpy as jnp
from jax import lax
from jax.experimental import pallas as pl
from jax.experimental.pallas import tpu as pltpu
from jax.sharding import PartitionSpec as P

MESH = pl.DeviceIdType.MESH
F32 = jnp.float32
BF16 = jnp.bfloat16
I32 = jnp.int32

SINKS = 4
FILL_LOW = -1e30
EPSILON = 1e-05
OUT_SCALE = 0.8
LOG2E = 1.4426950408889634

NC = 2
ROWS_DEV = 4
CHUNKS = 4
TILE = ROWS_DEV * CHUNKS
QK = 128
VD = 256
MSG = VD + 128


def nt(a, b):
    return lax.dot_general(a, b, (((1,), (1,)), ((), ())), preferred_element_type=F32)


def iota(shape, dim):
    return lax.broadcasted_iota(I32, shape, dim)


def slot_of(index, nx):
    row = index % ROWS_DEV
    zl = (index // TILE) % 2
    x = (index // (2 * TILE)) % nx
    core = index // (2 * TILE * nx)
    return ((zl * nx + x) * NC + core) * ROWS_DEV + row


def chunk_of(index):
    return (index // ROWS_DEV) % CHUNKS


def tile_of(ref):
    value = ref[...].astype(F32)
    pieces = [value[:, QK * c : QK * (c + 1)] for c in range(CHUNKS)]
    return jnp.concatenate(pieces, axis=0).astype(BF16)


def unpack(message):
    wide = message.astype(F32)
    shift = wide[:, VD : VD + 1]
    total = wide[:, VD + 1 : VD + 2] + wide[:, VD + 2 : VD + 3]
    return shift, total, wide[:, :VD]


def merge(parts):
    peak = functools.reduce(jnp.maximum, [p[0] for p in parts])
    factors = [jnp.exp2(p[0] - peak) for p in parts]
    total = sum(f * p[1] for f, p in zip(factors, parts))
    weighted = sum(f * p[2] for f, p in zip(factors, parts))
    return peak, total, weighted


def pack(part):
    shift, total, weighted = part
    rows = weighted.shape[0]
    high = total.astype(BF16).astype(F32)
    lane = iota((rows, 128), 1)
    stats = jnp.where(lane == 0, shift, jnp.where(lane == 1, high, total - high))
    return weighted.astype(BF16), stats.astype(BF16)


def attention_kernel(
    nz, nx, nh, window,
    lengths_in, draft_counts_in, lambdas_in, hidden_in, queries_in, keys_in, values_in, gain_in, parents_in,
    cache_k, cache_v, out_weight,
    mixed, kv_out,
    lengths, draft_counts, lambdas, hidden, queries, keys, values, gain, parents,
    gq, gkv, kc, vc, wv, tree, part, core_in, chip, x_in, plane, z_in, y_out, y_in,
    qz_s, qz_r, qx_s, qx_r, qc_s, qc_r, kz_s, kz_r, kx_s, kx_r, kc_s, kc_r,
    rc_s, rc_r, rx_s, rx_r, rz_s, rz_r, y_s, y_r, load_sem, w_sem, out_sem, small_sem,
):
    nr = nz // 2
    slots = 2 * nx * NC * ROWS_DEV
    span = cache_k.shape[2]
    rows = 2 * nx * NC * TILE
    seq = lax.axis_index("seq")
    head = lax.axis_index("head")
    core = seq % NC
    x = (seq // NC) % nx
    z = seq // (NC * nx)

    def device(zz, xx, cc):
        return ((zz * nx + xx) * NC + cc, head)

    def remote(src, dst, send, recv, target):
        return pltpu.make_async_remote_copy(
            src_ref=src, dst_ref=dst, send_sem=send, recv_sem=recv, device_id=target, device_id_type=MESH
        )

    z_peers = [(d, (z + d) % nz, (z + nz - d) % nz) for d in range(1, nz)]
    x_peers = [(d, (x + d) % nx, (x + nx - d) % nx) for d in range(1, nx)]
    h_peers = [(d, (head + d) % nh, (head + nh - d) % nh) for d in range(1, nh)]
    other = 1 - core

    barrier = pltpu.get_barrier_semaphore()
    peers = [device(z, x, other)]
    peers += [device(to, x, core) for _, to, _ in z_peers]
    peers += [device(z, to, core) for _, to, _ in x_peers]
    peers += [(seq, to) for _, to, _ in h_peers]
    for peer in peers:
        pl.semaphore_signal(barrier, inc=1, device_id=peer, device_id_type=MESH)

    small = [
        pltpu.make_async_copy(src, dst, small_sem.at[i])
        for i, (src, dst) in enumerate(
            [
                (queries_in, queries), (keys_in, keys), (values_in, values), (parents_in, parents), (lengths_in, lengths),
                (draft_counts_in, draft_counts), (lambdas_in, lambdas), (hidden_in, hidden), (gain_in, gain),
            ]
        )
    ]
    for copy in small:
        copy.start()
    loads = []
    for r in range(nr):
        loads.append(
            (
                pltpu.make_async_copy(cache_k.at[r], kc.at[r], load_sem.at[r, 0]),
                pltpu.make_async_copy(cache_v.at[r], vc.at[r], load_sem.at[r, 1]),
            )
        )
    for copy_k, copy_v in loads:
        copy_k.start()
        copy_v.start()
    load_w = pltpu.make_async_copy(out_weight, wv, w_sem)
    load_w.start()

    for copy in small:
        copy.wait()
    gq[core, x, z] = tile_of(queries)
    gkv[core, x, z, 0] = tile_of(keys)
    gkv[core, x, z, 1] = tile_of(values)

    pl.semaphore_wait(barrier, len(peers))

    sent = []

    def gather_z(buf, send, recv):
        waits = []
        for d, to, source in z_peers:
            copy = remote(buf.at[core, x, z], buf.at[core, x, z], send.at[d], recv.at[d], device(to, x, core))
            copy.start()
            sent.append(copy)
            waits.append(remote(buf.at[core, x, z], buf.at[core, x, source], send.at[d], recv.at[d], device(to, x, core)))
        return waits

    def gather_x(buf, send, recv):
        waits = []
        for d, to, source in x_peers:
            copy = remote(buf.at[core, x], buf.at[core, x], send.at[d], recv.at[d], device(z, to, core))
            copy.start()
            sent.append(copy)
            waits.append(remote(buf.at[core, x], buf.at[core, source], send.at[d], recv.at[d], device(z, to, core)))
        return waits

    def gather_core(buf, send, recv):
        copy = remote(buf.at[core], buf.at[core], send, recv, device(z, x, other))
        copy.start()
        sent.append(copy)
        return [remote(buf.at[core], buf.at[other], send, recv, device(z, x, other))]

    def arrived(waits):
        for copy in waits:
            copy.wait_recv()

    q_z = gather_z(gq, qz_s, qz_r)
    kv_z = gather_z(gkv, kz_s, kz_r)

    row_slot = slot_of(iota((rows, slots), 0), nx)
    row_pick = (row_slot == iota((rows, slots), 1)).astype(BF16)
    chunk = chunk_of(iota((rows, 1), 0))
    low = iota((slots, slots), 0)
    high = iota((slots, slots), 1)
    trees = []
    for r in range(nr):
        link = (low == parents[r : r + 1, :]) & (high >= 1)
        trees.append((link | (low == high)).astype(F32).astype(BF16))
    for _ in range(max(1, (slots - 1).bit_length())):
        trees = [jnp.minimum(jnp.dot(t, t, preferred_element_type=F32), 1.0).astype(BF16) for t in trees]
    oldest = []
    for r in range(nr):
        tree[r] = trees[r]
        depth = jnp.sum(nt(row_pick, trees[r]), axis=1, keepdims=True) - 1.0
        oldest.append(depth + (lengths[r] - window).astype(F32))

    arrived(q_z)
    q_x = gather_x(gq, qx_s, qx_r)
    arrived(q_x)
    q_c = gather_core(gq, qc_s, qc_r)
    arrived(kv_z)
    kv_x = gather_x(gkv, kx_s, kx_r)
    arrived(q_c)

    scale = LOG2E / math.sqrt(QK)
    position = (seq * span + iota((1, span), 1)).astype(F32)

    def attend(r):
        loads[r][0].wait()
        loads[r][1].wait()
        q = gq[:, :, 2 * r : 2 * r + 2].reshape(rows, QK)
        zero = jnp.zeros_like(q)
        split = [jnp.where(chunk == c, q, zero) for c in range(CHUNKS)]
        scores = nt(jnp.concatenate(split[:2], axis=1), kc[r, 0]) + nt(jnp.concatenate(split[2:], axis=1), kc[r, 1])
        reach = jnp.where(position < SINKS, -FILL_LOW, position)
        reach = jnp.where(position < lengths[r].astype(F32), reach, FILL_LOW)
        allowed = reach > oldest[r]
        scores = jnp.where(allowed, scores * scale, FILL_LOW)
        shift = jnp.max(scores, axis=1, keepdims=True).astype(BF16).astype(F32)
        weight = jnp.where(allowed, jnp.exp2(scores - shift), 0.0)
        total = jnp.sum(weight, axis=1, keepdims=True)
        weight = weight.astype(BF16)
        weighted = jnp.where(
            chunk < 2,
            jnp.dot(weight, vc[r, 0], preferred_element_type=F32),
            jnp.dot(weight, vc[r, 1], preferred_element_type=F32),
        )
        body, stats = pack((shift, total, weighted))
        part[r, :, :, :, :, :VD] = body.reshape(NC, nx, 2, TILE, VD)
        part[r, :, :, :, :, VD:] = stats.reshape(NC, nx, 2, TILE, 128)
        copy = remote(part.at[r, other], core_in.at[r], rc_s.at[r], rc_r.at[r], device(z, x, other))
        copy.start()
        sent.append(copy)
        return copy

    def chip_merge(r, copy):
        copy.wait_recv()
        block = nx * 2 * TILE
        mine = part[r, core].reshape(block, MSG)
        theirs = core_in[r].reshape(block, MSG)
        body, stats = pack(merge([unpack(mine), unpack(theirs)]))
        chip[r, :, :, :, :VD] = body.reshape(nx, 2, TILE, VD)
        chip[r, :, :, :, VD:] = stats.reshape(nx, 2, TILE, 128)
        waits = []
        for d, to, source in x_peers:
            copy = remote(chip.at[r, to], x_in.at[r, d], rx_s.at[r, d], rx_r.at[r, d], device(z, to, core))
            copy.start()
            sent.append(copy)
            waits.append(copy)
        return waits

    def plane_merge(r, waits):
        arrived(waits)
        parts = [unpack(chip[r, x].reshape(2 * TILE, MSG))]
        for d, _, _ in x_peers:
            parts.append(unpack(x_in[r, d].reshape(2 * TILE, MSG)))
        body, stats = pack(merge(parts))
        plane[r, :, :, :VD] = body.reshape(2, TILE, VD)
        plane[r, :, :, VD:] = stats.reshape(2, TILE, 128)
        for zl in range(2):
            to = 2 * r + zl

            @pl.when(z != to)
            def _():
                remote(plane.at[r, zl], z_in.at[z], rz_s.at[to], rz_r.at[z], device(to, x, core)).start()

            @pl.when(z == to)
            def _():
                z_in[z] = plane[r, zl]

    in_core = {}
    in_x = {}
    in_core[0] = attend(0)
    arrived(kv_x)
    kv_c = gather_core(gkv, kc_s, kc_r)
    for r in range(1, nr + 2):
        if r < nr:
            in_core[r] = attend(r)
        if r - 1 < nr:
            in_x[r - 1] = chip_merge(r - 1, in_core[r - 1])
        if r >= 2:
            plane_merge(r - 2, in_x[r - 2])

    arrived(kv_c)
    kv_copy = pltpu.make_async_copy(gkv, kv_out, out_sem)
    kv_copy.start()

    own = z // 2
    own_slot = ((z % 2) * nx + x) * NC + core
    own_slot = own_slot * ROWS_DEV
    keys_own = gkv[:, :, pl.ds(2 * own, 2), 0].reshape(rows, QK)
    values_own = gkv[:, :, pl.ds(2 * own, 2), 1].reshape(rows, QK)
    pick_row = (own_slot + iota((TILE, slots), 0) % ROWS_DEV == iota((TILE, slots), 1)).astype(BF16)
    live = (iota((TILE, slots), 1) < draft_counts[own]).astype(F32)
    seen = (nt(pick_row, tree[own]) * live).astype(BF16)
    pick_lane = (slot_of(iota((slots, rows), 1), nx) == iota((slots, rows), 0)).astype(BF16)
    lane_chunk = chunk_of(iota((TILE, rows), 1))
    row_chunk = iota((TILE, rows), 0) // ROWS_DEV
    allowed = (jnp.dot(seen, pick_lane, preferred_element_type=F32) > 0.5) & (lane_chunk == row_chunk)
    scores = jnp.where(allowed, nt(gq[core, x, z], keys_own) * scale, FILL_LOW)
    shift = jnp.max(scores, axis=1, keepdims=True)
    weight = jnp.where(allowed, jnp.exp2(scores - shift), 0.0)
    total = jnp.sum(weight, axis=1, keepdims=True)
    first_map = row_chunk % 2 == 0
    ahead = pltpu.roll(weight, ROWS_DEV, 1)
    behind = pltpu.roll(weight, rows - ROWS_DEV, 1)
    left = jnp.where(first_map, weight, behind).astype(BF16)
    right = jnp.where(first_map, ahead, weight).astype(BF16)
    weighted = jnp.concatenate(
        [
            jnp.dot(left, values_own, preferred_element_type=F32),
            jnp.dot(right, values_own, preferred_element_type=F32),
        ],
        axis=1,
    )
    draft = (shift, total, weighted)

    for d, to, source in z_peers:
        remote(plane.at[0, 0], z_in.at[source], rz_s.at[to], rz_r.at[source], device(to, x, core)).wait_recv()
    peak, total, weighted = merge([unpack(z_in[i]) for i in range(nz)] + [draft])
    attended = weighted / total
    row_live = own_slot + iota((ROWS_DEV, 1), 0) < draft_counts[own]
    normed = []
    for h in range(2):
        first = attended[2 * h * ROWS_DEV : (2 * h + 1) * ROWS_DEV]
        second = attended[(2 * h + 1) * ROWS_DEV : (2 * h + 2) * ROWS_DEV]
        difference = first - lambdas[h] * second
        square = jnp.mean(difference * difference, axis=1, keepdims=True)
        scaled = difference * lax.rsqrt(square + EPSILON) * gain[...] * OUT_SCALE
        normed.append(jnp.where(row_live, scaled, 0.0).astype(BF16))
    load_w.wait()
    product = jnp.dot(jnp.concatenate(normed, axis=1), wv[...], preferred_element_type=F32)
    width = mixed.shape[1]
    for h in range(nh):
        y_out[h] = product[:, h * width : (h + 1) * width]
    waits = []
    for d, to, source in h_peers:
        copy = remote(y_out.at[to], y_in.at[d], y_s.at[d], y_r.at[d], (seq, to))
        copy.start()
        sent.append(copy)
        waits.append(copy)
    summed = y_out[head]
    arrived(waits)
    for d, _, _ in h_peers:
        summed = summed + y_in[d]
    mixed[...] = (summed + hidden[...].astype(F32)).astype(BF16)

    for copy in sent:
        copy.wait_send()
    for d, to, source in z_peers:
        remote(plane.at[0, 0], z_in.at[source], rz_s.at[to], rz_r.at[source], device(to, x, core)).wait_send()
    kv_copy.wait()


def cache_kernel(
    nz, nx, lengths_in, count_in, path_in, mixed_in, kv, cache_k, cache_v, mixed, new_k, new_v,
    lengths, accepted_count, path, kvb, kb, vb, in_sem, out_sem, kv_sem, small_sem,
):
    nr = nz // 2
    slots = 2 * nx * NC * ROWS_DEV
    rows = 2 * nx * NC * TILE
    span = cache_k.shape[2]
    seq = lax.axis_index("seq")
    load_kv = pltpu.make_async_copy(kv, kvb, kv_sem)
    load_kv.start()
    pairs = ((cache_k, kb, new_k), (cache_v, vb, new_v))
    loads, stores = [], []
    for r in range(nr):
        loads.append([pltpu.make_async_copy(src.at[r], buf.at[r], in_sem.at[r, i]) for i, (src, buf, _) in enumerate(pairs)])
        stores.append([pltpu.make_async_copy(buf.at[r], dst.at[r], out_sem.at[r, i]) for i, (_, buf, dst) in enumerate(pairs)])
    for r in range(nr):
        for copy in loads[r]:
            copy.start()
    small = [
        pltpu.make_async_copy(src, dst, small_sem.at[i])
        for i, (src, dst) in enumerate([(lengths_in, lengths), (count_in, accepted_count), (path_in, path), (mixed_in, mixed)])
    ]
    for copy in small:
        copy.start()
    for copy in small:
        copy.wait()
    reach = slots + 16
    load_kv.wait()
    for r in range(nr):
        for copy in loads[r]:
            copy.wait()
        begin = lengths[r] - seq * span
        count = accepted_count[r]

        @pl.when((begin < span) & (begin + count > 0))
        def _():
            base = jnp.clip(begin // 16 * 16, 0, span - reach)
            base = pl.multiple_of(base, 16)
            place = iota((reach, slots), 0) + (base - begin)
            order = iota((reach, slots), 1)
            taken = ((place == order) & (order < count)).astype(BF16)
            source = (path[r : r + 1, :] == iota((slots, slots), 0)).astype(BF16)
            pick = nt(taken, source).astype(BF16)
            lanes = (slot_of(iota((slots, rows), 1), nx) == iota((slots, rows), 0)).astype(BF16)
            wide = jnp.dot(pick, lanes, preferred_element_type=F32)
            lane_chunk = chunk_of(iota((reach, rows), 1))
            row_place = iota((reach, 1), 0) + (base - begin)
            touched = (row_place >= 0) & (row_place < count)
            for i, (_, buf, _) in enumerate(pairs):
                block = kvb[:, :, 2 * r : 2 * r + 2, i].reshape(rows, 128)
                for c in range(CHUNKS):
                    chosen = jnp.where(lane_chunk == c, wide, 0.0).astype(BF16)
                    fresh = jnp.dot(chosen, block, preferred_element_type=F32)
                    where = (r, c // 2, pl.ds(base, reach), pl.ds(128 * (c % 2), 128))
                    old = buf[where].astype(F32)
                    buf[where] = jnp.where(touched, fresh, old).astype(BF16)

        for copy in stores[r]:
            copy.start()
    for r in range(nr):
        for copy in stores[r]:
            copy.wait()


def body(
    nz, nx, nh, window,
    hidden, draft_queries, draft_keys, draft_values, cache_k, cache_v, lambdas, norm_gain, out_weight,
    lengths, parents, draft_counts, accepted_path, accepted_count,
):
    nr = nz // 2
    slots = 2 * nx * NC * ROWS_DEV
    vmem = pl.BlockSpec(memory_space=pltpu.VMEM)
    hbm = pl.BlockSpec(memory_space=pltpu.MemorySpace.HBM)
    dma = pltpu.SemaphoreType.DMA
    kv_shape = (NC, nx, nz, 2, TILE, 128)
    mixed, kv = pl.pallas_call(
        functools.partial(attention_kernel, nz, nx, nh, window),
        out_shape=(jax.ShapeDtypeStruct(hidden.shape, BF16), jax.ShapeDtypeStruct(kv_shape, BF16)),
        in_specs=[hbm] * 12,
        out_specs=(vmem, hbm),
        scratch_shapes=[
            pltpu.SMEM(lengths.shape, I32),
            pltpu.SMEM(draft_counts.shape, I32),
            pltpu.SMEM(lambdas.shape, F32),
            pltpu.VMEM(hidden.shape, BF16),
            pltpu.VMEM(hidden.shape, BF16),
            pltpu.VMEM(hidden.shape, BF16),
            pltpu.VMEM(hidden.shape, BF16),
            pltpu.VMEM((1, VD), F32),
            pltpu.VMEM(parents.shape, I32),
            pltpu.VMEM((NC, nx, nz, TILE, 128), BF16),
            pltpu.VMEM(kv_shape, BF16),
            pltpu.VMEM(cache_k.shape, BF16),
            pltpu.VMEM(cache_v.shape, BF16),
            pltpu.VMEM(out_weight.shape, BF16),
            pltpu.VMEM((nr, slots, slots), BF16),
            pltpu.VMEM((nr, NC, nx, 2, TILE, MSG), BF16),
            pltpu.VMEM((nr, nx, 2, TILE, MSG), BF16),
            pltpu.VMEM((nr, nx, 2, TILE, MSG), BF16),
            pltpu.VMEM((nr, nx, 2, TILE, MSG), BF16),
            pltpu.VMEM((nr, 2, TILE, MSG), BF16),
            pltpu.VMEM((nz, TILE, MSG), BF16),
            pltpu.VMEM((nh, ROWS_DEV, hidden.shape[1]), F32),
            pltpu.VMEM((nh, ROWS_DEV, hidden.shape[1]), F32),
            dma((nz,)), dma((nz,)), dma((nx,)), dma((nx,)), dma, dma,
            dma((nz,)), dma((nz,)), dma((nx,)), dma((nx,)), dma, dma,
            dma((nr,)), dma((nr,)), dma((nr, nx)), dma((nr, nx)), dma((nz,)), dma((nz,)), dma((nh,)), dma((nh,)),
            dma((nr, 2)), dma, dma, dma((9,)),
        ],
        compiler_params=pltpu.CompilerParams(collective_id=0, has_side_effects=True, vmem_limit_bytes=60 << 20),
    )(
        lengths, draft_counts, lambdas, hidden, draft_queries, draft_keys, draft_values,
        norm_gain.reshape(1, VD), parents, cache_k, cache_v, out_weight,
    )
    return pl.pallas_call(
        functools.partial(cache_kernel, nz, nx),
        out_shape=(
            jax.ShapeDtypeStruct(hidden.shape, BF16),
            jax.ShapeDtypeStruct(cache_k.shape, BF16),
            jax.ShapeDtypeStruct(cache_v.shape, BF16),
        ),
        in_specs=[hbm] * 7,
        out_specs=(hbm, hbm, hbm),
        scratch_shapes=[
            pltpu.SMEM(lengths.shape, I32),
            pltpu.SMEM(accepted_count.shape, I32),
            pltpu.VMEM(accepted_path.shape, I32),
            pltpu.VMEM(kv_shape, BF16),
            pltpu.VMEM(cache_k.shape, BF16),
            pltpu.VMEM(cache_v.shape, BF16),
            dma((nr, 2)), dma((nr, 2)), dma, dma((4,)),
        ],
        compiler_params=pltpu.CompilerParams(vmem_limit_bytes=60 << 20),
    )(lengths, accepted_count, accepted_path, mixed, kv, cache_k, cache_v)


def build(mesh, nz, nx, window):
    seq_rows = P("seq", "head")
    cache = P(None, "head", "seq", None)
    in_specs = (seq_rows,) * 4 + (cache, cache, P("head"), P(), P("head", None)) + (P(),) * 5
    return jax.shard_map(
        functools.partial(body, nz, nx, mesh.shape["head"], window),
        mesh=mesh,
        in_specs=in_specs,
        out_specs=(seq_rows, cache, cache),
        check_vma=False,
    )


def solution(mesh):
    return build(mesh, 8, 4, 4096)
```

```python
import functools
import math

import jax
import jax.numpy as jnp
from jax import lax
from jax.experimental import pallas as pl
from jax.experimental.pallas import tpu as pltpu
from jax.sharding import PartitionSpec as P

MESH = pl.DeviceIdType.MESH
F32 = jnp.float32
BF16 = jnp.bfloat16
I32 = jnp.int32

SINKS = 4
FILL_LOW = -1e30
EPSILON = 1e-05
OUT_SCALE = 0.8
LOG2E = 1.4426950408889634

STAGED = (0, 1, 2)
NC = 2
ROWS_DEV = 4
CHUNKS = 4
TILE = ROWS_DEV * CHUNKS
QK = 128
VD = 256
MSG = VD + 128


def nt(a, b):
    return lax.dot_general(a, b, (((1,), (1,)), ((), ())), preferred_element_type=F32)


def iota(shape, dim):
    return lax.broadcasted_iota(I32, shape, dim)


def slot_of(index, nx):
    row = index % ROWS_DEV
    zl = (index // TILE) % 2
    x = (index // (2 * TILE)) % nx
    core = index // (2 * TILE * nx)
    return ((zl * nx + x) * NC + core) * ROWS_DEV + row


def chunk_of(index):
    return (index // ROWS_DEV) % CHUNKS


def tile_of(ref):
    value = ref[...].astype(F32)
    pieces = [value[:, QK * c : QK * (c + 1)] for c in range(CHUNKS)]
    return jnp.concatenate(pieces, axis=0).astype(BF16)


def unpack(message):
    wide = message.astype(F32)
    shift = wide[:, VD : VD + 1]
    total = wide[:, VD + 1 : VD + 2] + wide[:, VD + 2 : VD + 3]
    return shift, total, wide[:, :VD]


def merge(parts):
    peak = functools.reduce(jnp.maximum, [p[0] for p in parts])
    factors = [jnp.exp2(p[0] - peak) for p in parts]
    total = sum(f * p[1] for f, p in zip(factors, parts))
    weighted = sum(f * p[2] for f, p in zip(factors, parts))
    return peak, total, weighted


def pack(part):
    shift, total, weighted = part
    rows = weighted.shape[0]
    high = total.astype(BF16).astype(F32)
    lane = iota((rows, 128), 1)
    stats = jnp.where(lane == 0, shift, jnp.where(lane == 1, high, total - high))
    return weighted.astype(BF16), stats.astype(BF16)


def attention_kernel(
    nz, nx, nh, window,
    lengths_in, draft_counts_in, lambdas_in, hidden_in, queries_in, keys_in, values_in, gain_in, parents_in,
    path_in, accepted_in, cache_k, cache_v, out_weight,
    mixed, kc, vc,
    path, accepted, lengths, draft_counts, lambdas, hidden, queries, keys, values, gain, parents,
    gq, gkv, wv, tree, oldest, part, core_in, chip, x_in, plane, z_in, y_out, y_in,
    qz_s, qz_r, qx_s, qx_r, qc_s, qc_r, kz_s, kz_r, kx_s, kx_r, kc_s, kc_r,
    rc_s, rc_r, rx_s, rx_r, rz_s, rz_r, y_s, y_r, load_sem, w_sem, small_sem,
):
    nr = nz // 2
    slots = 2 * nx * NC * ROWS_DEV
    span = cache_k.shape[2]
    rows = 2 * nx * NC * TILE
    seq = lax.axis_index("seq")
    head = lax.axis_index("head")
    core = seq % NC
    x = (seq // NC) % nx
    z = seq // (NC * nx)

    def device(zz, xx, cc):
        return ((zz * nx + xx) * NC + cc, head)

    def remote(src, dst, send, recv, target):
        return pltpu.make_async_remote_copy(
            src_ref=src, dst_ref=dst, send_sem=send, recv_sem=recv, device_id=target, device_id_type=MESH
        )

    z_peers = [(d, (z + d) % nz, (z + nz - d) % nz) for d in range(1, nz)]
    x_peers = [(d, (x + d) % nx, (x + nx - d) % nx) for d in range(1, nx)]
    h_peers = [(d, (head + d) % nh, (head + nh - d) % nh) for d in range(1, nh)]
    other = 1 - core
    own = z // 2
    even = 1 - z % 2
    order = [(own + nr // 2) % nr, (own + nr - 1 + 2 * even) % nr, (own + nr + 1 - 2 * even) % nr, own]
    last = len(order) - 1

    barrier = pltpu.get_barrier_semaphore()
    peers = [device(z, x, other)]
    peers += [device(to, x, core) for _, to, _ in z_peers]
    peers += [device(z, to, core) for _, to, _ in x_peers]
    peers += [(seq, to) for _, to, _ in h_peers]
    for peer in peers:
        pl.semaphore_signal(barrier, inc=1, device_id=peer, device_id_type=MESH)

    small = [
        pltpu.make_async_copy(src, dst, small_sem.at[i])
        for i, (src, dst) in enumerate(
            [
                (queries_in, queries), (keys_in, keys), (values_in, values), (parents_in, parents), (lengths_in, lengths),
                (path_in, path), (accepted_in, accepted), (draft_counts_in, draft_counts), (lambdas_in, lambdas), (hidden_in, hidden), (gain_in, gain),
            ]
        )
    ]
    for copy in small:
        copy.start()
    loads = []
    for r in range(nr):
        loads.append(
            (
                pltpu.make_async_copy(cache_k.at[r], kc.at[r], load_sem.at[r, 0]),
                pltpu.make_async_copy(cache_v.at[r], vc.at[r], load_sem.at[r, 1]),
            )
        )
    for copy_k, copy_v in loads:
        copy_k.start()
        copy_v.start()
    load_w = pltpu.make_async_copy(out_weight, wv, w_sem)
    load_w.start()

    for copy in small:
        copy.wait()
    gq[core, x, z] = tile_of(queries)
    gkv[core, x, z, 0] = tile_of(keys)
    gkv[core, x, z, 1] = tile_of(values)

    pl.semaphore_wait(barrier, len(peers))

    sent = []

    def gather_z(buf, send, recv):
        waits = []
        for d, to, source in z_peers:
            copy = remote(buf.at[core, x, z], buf.at[core, x, z], send.at[d], recv.at[d], device(to, x, core))
            copy.start()
            sent.append(copy)
            waits.append(remote(buf.at[core, x, z], buf.at[core, x, source], send.at[d], recv.at[d], device(to, x, core)))
        return waits

    def gather_x(buf, send, recv):
        waits = []
        for d, to, source in x_peers:
            copy = remote(buf.at[core, x], buf.at[core, x], send.at[d], recv.at[d], device(z, to, core))
            copy.start()
            sent.append(copy)
            waits.append(remote(buf.at[core, x], buf.at[core, source], send.at[d], recv.at[d], device(z, to, core)))
        return waits

    def gather_core(buf, send, recv):
        copy = remote(buf.at[core], buf.at[core], send, recv, device(z, x, other))
        copy.start()
        sent.append(copy)
        return [remote(buf.at[core], buf.at[other], send, recv, device(z, x, other))]

    def arrived(waits):
        for copy in waits:
            copy.wait_recv()

    q_z = gather_z(gq, qz_s, qz_r)
    kv_z = gather_z(gkv, kz_s, kz_r)

    row_slot = slot_of(iota((rows, slots), 0), nx)
    row_pick = (row_slot == iota((rows, slots), 1)).astype(BF16)
    chunk = chunk_of(iota((rows, 1), 0))
    low = iota((slots, slots), 0)
    high = iota((slots, slots), 1)
    trees = []
    for r in range(nr):
        link = (low == parents[r : r + 1, :]) & (high >= 1)
        trees.append((link | (low == high)).astype(F32).astype(BF16))
    for _ in range(max(1, (slots - 1).bit_length())):
        trees = [jnp.minimum(jnp.dot(t, t, preferred_element_type=F32), 1.0).astype(BF16) for t in trees]
    for r in range(nr):
        tree[r] = trees[r]
        depth = jnp.sum(nt(row_pick, trees[r]), axis=1, keepdims=True) - 1.0
        oldest[r] = depth + (lengths[r] - window).astype(F32)

    arrived(q_z)
    q_x = gather_x(gq, qx_s, qx_r)
    arrived(q_x)
    q_c = gather_core(gq, qc_s, qc_r)
    arrived(kv_z)
    kv_x = gather_x(gkv, kx_s, kx_r)
    arrived(q_c)

    scale = LOG2E / math.sqrt(QK)
    position = (seq * span + iota((1, span), 1)).astype(F32)

    def attend(k):
        r = order[k]
        q = gq[:, :, pl.ds(2 * r, 2)].reshape(rows, QK)
        zero = jnp.zeros_like(q)
        split = [jnp.where(chunk == c, q, zero) for c in range(CHUNKS)]
        scores = nt(jnp.concatenate(split[:2], axis=1), kc[r, 0]) + nt(jnp.concatenate(split[2:], axis=1), kc[r, 1])
        reach = jnp.where(position < SINKS, -FILL_LOW, position)
        reach = jnp.where(position < lengths[r].astype(F32), reach, FILL_LOW)
        allowed = reach > oldest[r]
        scores = jnp.where(allowed, scores * scale, FILL_LOW)
        shift = jnp.max(scores, axis=1, keepdims=True).astype(BF16).astype(F32)
        weight = jnp.where(allowed, jnp.exp2(scores - shift), 0.0)
        total = jnp.sum(weight, axis=1, keepdims=True)
        weight = weight.astype(BF16)
        weighted = jnp.where(
            chunk < 2,
            jnp.dot(weight, vc[r, 0], preferred_element_type=F32),
            jnp.dot(weight, vc[r, 1], preferred_element_type=F32),
        )
        body, stats = pack((shift, total, weighted))
        part[k, :, :, :, :, :VD] = body.reshape(NC, nx, 2, TILE, VD)
        part[k, :, :, :, :, VD:] = stats.reshape(NC, nx, 2, TILE, 128)
        copy = remote(part.at[k, other], core_in.at[k], rc_s.at[k], rc_r.at[k], device(z, x, other))
        copy.start()
        sent.append(copy)
        return copy

    def chip_merge(k, copy):
        copy.wait_recv()
        block = nx * 2 * TILE
        mine = part[k, core].reshape(block, MSG)
        theirs = core_in[k].reshape(block, MSG)
        body, stats = pack(merge([unpack(mine), unpack(theirs)]))
        chip[k, :, :, :, :VD] = body.reshape(nx, 2, TILE, VD)
        chip[k, :, :, :, VD:] = stats.reshape(nx, 2, TILE, 128)

    def send_x(k):
        waits = []
        for d, to, source in x_peers:
            copy = remote(chip.at[k, to], x_in.at[k, d], rx_s.at[k, d], rx_r.at[k, d], device(z, to, core))
            copy.start()
            sent.append(copy)
            waits.append(copy)
        return waits

    def to_owner(src, k, zl, d, zz, xx):
        copy = remote(src, z_in.at[z, x], rz_s.at[k, zl, d], rz_r.at[z, x], device(zz, xx, core))
        copy.start()
        sent.append(copy)

    def plane_merge(k, waits):
        arrived(waits)
        parts = [unpack(chip[k, x].reshape(2 * TILE, MSG))]
        for d, _, _ in x_peers:
            parts.append(unpack(x_in[k, d].reshape(2 * TILE, MSG)))
        body, stats = pack(merge(parts))
        plane[k, :, :, :VD] = body.reshape(2, TILE, VD)
        plane[k, :, :, VD:] = stats.reshape(2, TILE, 128)
        if k == last:
            to_owner(plane.at[k, 1 - z % 2], k, 0, 0, z + 2 * even - 1, x)
            z_in[z, x] = plane[k, z % 2]
            return
        for zl in range(2):
            to_owner(plane.at[k, zl], k, zl, 0, 2 * order[k] + zl, x)

    def send_direct(k):
        if k < last:
            for d in range(nx - 1, -1, -1):
                for zl in range(2):
                    xx = (x + d) % nx
                    to_owner(chip.at[k, xx, zl], k, zl, d, 2 * order[k] + zl, xx)
            return
        mate = z + 2 * even - 1
        for d in range(nx - 1, -1, -1):
            xx = (x + d) % nx
            to_owner(chip.at[k, xx, mate % 2], k, 0, d, mate, xx)
            if d > 0:
                to_owner(chip.at[k, xx, z % 2], k, 1, d, z, xx)
        z_in[z, x] = chip[k, x, z % 2]

    for pair in loads:
        for copy in pair:
            copy.wait()
    in_core, in_x = {}, {}

    def spread(k):
        chip_merge(k, in_core[k])
        if k in STAGED:
            in_x[k] = send_x(k)
        else:
            send_direct(k)

    def settle(k):
        if k in STAGED:
            plane_merge(k, in_x[k])

    in_core[0] = attend(0)
    in_core[1] = attend(1)
    spread(0)
    in_core[2] = attend(2)
    spread(1)
    in_core[3] = attend(3)
    spread(2)
    settle(0)
    spread(3)
    arrived(kv_x)
    kv_c = gather_core(gkv, kc_s, kc_r)
    settle(1)
    settle(2)
    settle(3)
    arrived(kv_c)
    row_chunk_lane = chunk_of(iota((slots, rows), 1))
    slot_lane = slot_of(iota((slots, rows), 1), nx)

    def write(r):
        begin = lengths[r] - seq * span
        taken = (iota((span, slots), 0) - begin == iota((span, slots), 1)) & (iota((span, slots), 1) < accepted[r])
        taken = taken.astype(BF16)
        place = iota((span, 1), 0) - begin
        touched = (place >= 0) & (place < accepted[r])
        slot_order = (path[r : r + 1, :] == iota((slots, slots), 0)).astype(BF16)
        lanes = (slot_lane == iota((slots, rows), 0)).astype(BF16)
        wide = lax.dot_general(slot_order, lanes, (((0,), (0,)), ((), ())), preferred_element_type=F32)
        for i, buf in enumerate((kc, vc)):
            block = gkv[:, :, 2 * r : 2 * r + 2, i].reshape(rows, 128)
            for h in range(2):
                kept = [
                    jnp.dot(
                        jnp.where(row_chunk_lane == 2 * h + half, wide, 0.0).astype(BF16), block, preferred_element_type=F32
                    ).astype(BF16)
                    for half in range(2)
                ]
                fresh = jnp.dot(taken, jnp.concatenate(kept, axis=1), preferred_element_type=F32)
                buf[r, h] = jnp.where(touched, fresh, buf[r, h].astype(F32)).astype(BF16)

    for r in range(nr):
        write(r)

    own_slot = ((z % 2) * nx + x) * NC + core
    own_slot = own_slot * ROWS_DEV
    keys_own = gkv[:, :, pl.ds(2 * own, 2), 0].reshape(rows, QK)
    values_own = gkv[:, :, pl.ds(2 * own, 2), 1].reshape(rows, QK)
    pick_row = (own_slot + iota((TILE, slots), 0) % ROWS_DEV == iota((TILE, slots), 1)).astype(BF16)
    live = (iota((TILE, slots), 1) < draft_counts[own]).astype(F32)
    seen = (nt(pick_row, tree[own]) * live).astype(BF16)
    pick_lane = (slot_of(iota((slots, rows), 1), nx) == iota((slots, rows), 0)).astype(BF16)
    lane_chunk = chunk_of(iota((TILE, rows), 1))
    row_chunk = iota((TILE, rows), 0) // ROWS_DEV
    allowed = (jnp.dot(seen, pick_lane, preferred_element_type=F32) > 0.5) & (lane_chunk == row_chunk)
    scores = jnp.where(allowed, nt(gq[core, x, z], keys_own) * scale, FILL_LOW)
    shift = jnp.max(scores, axis=1, keepdims=True)
    weight = jnp.where(allowed, jnp.exp2(scores - shift), 0.0)
    total = jnp.sum(weight, axis=1, keepdims=True)
    first_map = row_chunk % 2 == 0
    ahead = pltpu.roll(weight, ROWS_DEV, 1)
    behind = pltpu.roll(weight, rows - ROWS_DEV, 1)
    left = jnp.where(first_map, weight, behind).astype(BF16)
    right = jnp.where(first_map, ahead, weight).astype(BF16)
    weighted = jnp.concatenate(
        [
            jnp.dot(left, values_own, preferred_element_type=F32),
            jnp.dot(right, values_own, preferred_element_type=F32),
        ],
        axis=1,
    )
    draft = (shift, total, weighted)

    parts = [draft, unpack(z_in[z, x])]

    def take(zz, xx):
        remote(plane.at[0, 0], z_in.at[zz, xx], rz_s.at[0, 0, 0], rz_r.at[zz, xx], device(zz, xx, core)).wait_recv()
        parts.append(unpack(z_in[zz, xx]))

    for step in range(2, nz):
        source = (2 * own + step) % nz
        rank = {nz // 2: 0, nz // 2 + 1: 0, nz // 2 - 1: 1, nz - 2: 1}.get(step, 2)
        if rank in STAGED:
            take(source, x)
        else:
            for xx in range(nx):
                take(source, xx)
    for d in range(nx):
        if last not in STAGED:
            take(z + 2 * even - 1, (x + d) % nx)
            if d > 0:
                take(z, (x + d) % nx)
        elif d == 0:
            take(z + 2 * even - 1, x)
    peak, total, weighted = merge(parts)
    attended = weighted / total
    row_live = own_slot + iota((ROWS_DEV, 1), 0) < draft_counts[own]
    normed = []
    for h in range(2):
        first = attended[2 * h * ROWS_DEV : (2 * h + 1) * ROWS_DEV]
        second = attended[(2 * h + 1) * ROWS_DEV : (2 * h + 2) * ROWS_DEV]
        difference = first - lambdas[h] * second
        square = jnp.mean(difference * difference, axis=1, keepdims=True)
        scaled = difference * lax.rsqrt(square + EPSILON) * gain[...] * OUT_SCALE
        normed.append(jnp.where(row_live, scaled, 0.0).astype(BF16))
    load_w.wait()
    product = jnp.dot(jnp.concatenate(normed, axis=1), wv[...], preferred_element_type=F32)
    width = mixed.shape[1]
    for h in range(nh):
        y_out[h] = product[:, h * width : (h + 1) * width]
    waits = []
    for d, to, source in h_peers:
        copy = remote(y_out.at[to], y_in.at[d], y_s.at[d], y_r.at[d], (seq, to))
        copy.start()
        sent.append(copy)
        waits.append(copy)
    for copy in sent[: -len(waits)] if waits else sent:
        copy.wait_send()
    summed = y_out[head]
    arrived(waits)
    for d, _, _ in h_peers:
        summed = summed + y_in[d]
    mixed[...] = (summed + hidden[...].astype(F32)).astype(BF16)

    for copy in waits:
        copy.wait_send()


def store_kernel(nr, mixed_in, kc, vc, mixed, new_k, new_v, sem):
    copies = []
    for r in range(nr):
        copies.append(pltpu.make_async_copy(kc.at[r], new_k.at[r], sem.at[2 * r]))
        copies.append(pltpu.make_async_copy(vc.at[r], new_v.at[r], sem.at[2 * r + 1]))
    copies.append(pltpu.make_async_copy(mixed_in, mixed, sem.at[2 * nr]))
    for copy in copies:
        copy.start()
    for copy in copies:
        copy.wait()


def body(
    nz, nx, nh, window,
    hidden, draft_queries, draft_keys, draft_values, cache_k, cache_v, lambdas, norm_gain, out_weight,
    lengths, parents, draft_counts, accepted_path, accepted_count,
):
    nr = nz // 2
    slots = 2 * nx * NC * ROWS_DEV
    rows = 2 * nx * NC * TILE
    vmem = pl.BlockSpec(memory_space=pltpu.VMEM)
    hbm = pl.BlockSpec(memory_space=pltpu.MemorySpace.HBM)
    dma = pltpu.SemaphoreType.DMA
    kv_shape = (NC, nx, nz, 2, TILE, 128)
    to_hbm = [
        pltpu.with_memory_space_constraint(a, pltpu.MemorySpace.HBM)
        for a in (
            lengths, draft_counts, lambdas, hidden, draft_queries, draft_keys, draft_values,
            norm_gain.reshape(1, VD), parents, accepted_path, accepted_count, cache_k, cache_v, out_weight,
        )
    ]
    mixed, kc, vc = pl.pallas_call(
        functools.partial(attention_kernel, nz, nx, nh, window),
        out_shape=(pltpu.VMEM(hidden.shape, BF16), pltpu.VMEM(cache_k.shape, BF16), pltpu.VMEM(cache_v.shape, BF16)),
        in_specs=[hbm] * 14,
        out_specs=(vmem, vmem, vmem),
        scratch_shapes=[
            pltpu.VMEM(accepted_path.shape, I32),
            pltpu.SMEM(accepted_count.shape, I32),
            pltpu.SMEM(lengths.shape, I32),
            pltpu.SMEM(draft_counts.shape, I32),
            pltpu.SMEM(lambdas.shape, F32),
            pltpu.VMEM(hidden.shape, BF16),
            pltpu.VMEM(hidden.shape, BF16),
            pltpu.VMEM(hidden.shape, BF16),
            pltpu.VMEM(hidden.shape, BF16),
            pltpu.VMEM((1, VD), F32),
            pltpu.VMEM(parents.shape, I32),
            pltpu.VMEM((NC, nx, nz, TILE, 128), BF16),
            pltpu.VMEM(kv_shape, BF16),
            pltpu.VMEM(out_weight.shape, BF16),
            pltpu.VMEM((nr, slots, slots), BF16),
            pltpu.VMEM((nr, rows, 1), F32),
            pltpu.VMEM((nr, NC, nx, 2, TILE, MSG), BF16),
            pltpu.VMEM((nr, nx, 2, TILE, MSG), BF16),
            pltpu.VMEM((nr, nx, 2, TILE, MSG), BF16),
            pltpu.VMEM((nr, nx, 2, TILE, MSG), BF16),
            pltpu.VMEM((nr, 2, TILE, MSG), BF16),
            pltpu.VMEM((nz, nx, TILE, MSG), BF16),
            pltpu.VMEM((nh, ROWS_DEV, hidden.shape[1]), F32),
            pltpu.VMEM((nh, ROWS_DEV, hidden.shape[1]), F32),
            dma((nz,)), dma((nz,)), dma((nx,)), dma((nx,)), dma, dma,
            dma((nz,)), dma((nz,)), dma((nx,)), dma((nx,)), dma, dma,
            dma((nr,)), dma((nr,)), dma((nr, nx)), dma((nr, nx)), dma((nr, 2, nx)), dma((nz, nx)), dma((nh,)), dma((nh,)),
            dma((nr, 2)), dma, dma((11,)),
        ],
        compiler_params=pltpu.CompilerParams(collective_id=0, has_side_effects=True, vmem_limit_bytes=48 << 20),
    )(*to_hbm)
    return pl.pallas_call(
        functools.partial(store_kernel, nr),
        out_shape=(
            jax.ShapeDtypeStruct(hidden.shape, BF16),
            jax.ShapeDtypeStruct(cache_k.shape, BF16),
            jax.ShapeDtypeStruct(cache_v.shape, BF16),
        ),
        in_specs=[vmem] * 3,
        out_specs=(hbm, hbm, hbm),
        scratch_shapes=[dma((2 * nr + 1,))],
        compiler_params=pltpu.CompilerParams(vmem_limit_bytes=2 << 20),
    )(*[pltpu.with_memory_space_constraint(a, pltpu.MemorySpace.VMEM) for a in (mixed, kc, vc)])


def build(mesh, nz, nx, window):
    seq_rows = P("seq", "head")
    cache = P(None, "head", "seq", None)
    in_specs = (seq_rows,) * 4 + (cache, cache, P("head"), P(), P("head", None)) + (P(),) * 5
    return jax.shard_map(
        functools.partial(body, nz, nx, mesh.shape["head"], window),
        mesh=mesh,
        in_specs=in_specs,
        out_specs=(seq_rows, cache, cache),
        check_vma=False,
    )


def solution(mesh):
    return build(mesh, 8, 4, 4096)
```

```python
import functools
import math

import jax
import jax.numpy as jnp
from jax import lax
from jax.experimental import pallas as pl
from jax.experimental.pallas import tpu as pltpu
from jax.sharding import PartitionSpec as P

MESH = pl.DeviceIdType.MESH
F32 = jnp.float32
BF16 = jnp.bfloat16
I32 = jnp.int32

SINKS = 4
FILL_LOW = -1e30
EPSILON = 1e-05
OUT_SCALE = 0.8
LOG2E = 1.4426950408889634

STAGED = (0, 1, 2)
NC = 2
ROWS_DEV = 4
CHUNKS = 4
TILE = ROWS_DEV * CHUNKS
QK = 128
VD = 256
MSG = VD + 128


def nt(a, b):
    return lax.dot_general(a, b, (((1,), (1,)), ((), ())), preferred_element_type=F32)


def iota(shape, dim):
    return lax.broadcasted_iota(I32, shape, dim)


def slot_of(index, nx):
    row = index % ROWS_DEV
    zl = (index // TILE) % 2
    x = (index // (2 * TILE)) % nx
    core = index // (2 * TILE * nx)
    return ((zl * nx + x) * NC + core) * ROWS_DEV + row


def chunk_of(index):
    return (index // ROWS_DEV) % CHUNKS


def tile_of(ref):
    value = ref[...].astype(F32)
    pieces = [value[:, QK * c : QK * (c + 1)] for c in range(CHUNKS)]
    return jnp.concatenate(pieces, axis=0).astype(BF16)


def unpack(message):
    wide = message.astype(F32)
    shift = wide[:, VD : VD + 1]
    total = wide[:, VD + 1 : VD + 2] + wide[:, VD + 2 : VD + 3]
    return shift, total, wide[:, :VD]


def merge(parts):
    peak = functools.reduce(jnp.maximum, [p[0] for p in parts])
    factors = [jnp.exp2(p[0] - peak) for p in parts]
    total = sum(f * p[1] for f, p in zip(factors, parts))
    weighted = sum(f * p[2] for f, p in zip(factors, parts))
    return peak, total, weighted


def stat_lanes(shift, total):
    high = total.astype(BF16).astype(F32)
    lane = iota((shift.shape[0], 128), 1)
    return jnp.where(lane == 0, shift, jnp.where(lane == 1, high, total - high))


def pack(part):
    shift, total, weighted = part
    return weighted.astype(BF16), stat_lanes(shift, total).astype(BF16)


def attention_kernel(
    nz, nx, nh, window,
    lengths_in, draft_counts_in, lambdas_in, hidden_in, queries_in, keys_in, values_in, gain_in, parents_in,
    path_in, accepted_in, cache_k, cache_v, out_weight,
    mixed, kc, vc,
    path, accepted, lengths, draft_counts, lambdas, hidden, queries, keys, values, gain, parents,
    gq, gkv, wv, tree, oldest, part, core_in, chip, x_in, plane, z_in, y_out, y_in,
    qz_s, qz_r, qx_s, qx_r, qc_s, qc_r, kz_s, kz_r, kx_s, kx_r, kc_s, kc_r,
    rc_s, rc_r, rx_s, rx_r, rz_s, rz_r, y_s, y_r, load_sem, w_sem, small_sem,
):
    nr = nz // 2
    slots = 2 * nx * NC * ROWS_DEV
    span = cache_k.shape[2]
    rows = 2 * nx * NC * TILE
    head_rows = rows // 2
    seq = lax.axis_index("seq")
    head = lax.axis_index("head")
    core = seq % NC
    x = (seq // NC) % nx
    z = seq // (NC * nx)

    def device(zz, xx, cc):
        return ((zz * nx + xx) * NC + cc, head)

    def remote(src, dst, send, recv, target):
        return pltpu.make_async_remote_copy(
            src_ref=src, dst_ref=dst, send_sem=send, recv_sem=recv, device_id=target, device_id_type=MESH
        )

    z_peers = [(d, (z + d) % nz, (z + nz - d) % nz) for d in range(1, nz)]
    x_peers = [(d, (x + d) % nx, (x + nx - d) % nx) for d in range(1, nx)]
    h_peers = [(d, (head + d) % nh, (head + nh - d) % nh) for d in range(1, nh)]
    other = 1 - core
    own = z // 2
    even = 1 - z % 2
    order = [(own + nr // 2) % nr, (own + nr - 1 + 2 * even) % nr, (own + nr + 1 - 2 * even) % nr, own]
    last = len(order) - 1

    small = [
        pltpu.make_async_copy(src, dst, small_sem.at[i])
        for i, (src, dst) in enumerate(
            [
                (queries_in, queries), (keys_in, keys), (values_in, values), (parents_in, parents), (lengths_in, lengths),
                (path_in, path), (accepted_in, accepted), (draft_counts_in, draft_counts), (lambdas_in, lambdas), (hidden_in, hidden), (gain_in, gain),
            ]
        )
    ]
    small[0].start()
    barrier = pltpu.get_barrier_semaphore()
    peers = [device(z, x, other)]
    peers += [device(to, x, core) for _, to, _ in z_peers]
    peers += [device(z, to, core) for _, to, _ in x_peers]
    peers += [device((z + dz) % nz, (x + dx) % nx, core) for dz in range(1, nz) for dx in range(1, nx)]
    peers += [(seq, to) for _, to, _ in h_peers]
    for peer in peers:
        pl.semaphore_signal(barrier, inc=1, device_id=peer, device_id_type=MESH)

    loads = []
    for r in range(nr):
        loads.append(
            (
                pltpu.make_async_copy(cache_k.at[r], kc.at[r], load_sem.at[r, 0]),
                pltpu.make_async_copy(cache_v.at[r], vc.at[r], load_sem.at[r, 1]),
            )
        )
    load_w = pltpu.make_async_copy(out_weight, wv, w_sem)
    for copy in small[1:]:
        copy.start()
    small[0].wait()
    gq[core, x, z] = tile_of(queries)

    pl.semaphore_wait(barrier, len(peers))

    sent = []

    def gather_z(buf, send, recv):
        waits = []
        for d, to, source in z_peers:
            copy = remote(buf.at[core, x, z], buf.at[core, x, z], send.at[d], recv.at[d], device(to, x, core))
            copy.start()
            sent.append(copy)
            waits.append(remote(buf.at[core, x, z], buf.at[core, x, source], send.at[d], recv.at[d], device(to, x, core)))
        return waits

    def gather_x(buf, send, recv):
        waits = []
        for d, to, source in x_peers:
            copy = remote(buf.at[core, x], buf.at[core, x], send.at[d], recv.at[d], device(z, to, core))
            copy.start()
            sent.append(copy)
            waits.append(remote(buf.at[core, x], buf.at[core, source], send.at[d], recv.at[d], device(z, to, core)))
        return waits

    def gather_core(buf, send, recv):
        copy = remote(buf.at[core], buf.at[core], send, recv, device(z, x, other))
        copy.start()
        sent.append(copy)
        return [remote(buf.at[core], buf.at[other], send, recv, device(z, x, other))]

    def arrived(waits):
        for copy in waits:
            copy.wait_recv()

    q_all = []
    for dz in sorted(range(nz), key=lambda i: -min(i, nz - i)):
        for dx in sorted(range(nx), key=lambda i: -min(i, nx - i)):
            if dz + dx > 0:
                mine = gq.at[core, x, z]
                target = device((z + dz) % nz, (x + dx) % nx, core)
                copy = remote(mine, mine, qz_s.at[dz, dx], qz_r.at[dz, dx], target)
                copy.start()
                sent.append(copy)
                theirs = gq.at[core, (x + nx - dx) % nx, (z + nz - dz) % nz]
                q_all.append(remote(mine, theirs, qz_s.at[dz, dx], qz_r.at[dz, dx], target))
    for copy_k, copy_v in loads:
        copy_k.start()
        copy_v.start()
    load_w.start()
    for copy in small[1:]:
        copy.wait()
    gkv[core, x, z, 0] = tile_of(keys)
    gkv[core, x, z, 1] = tile_of(values)
    kv_z = gather_z(gkv, kz_s, kz_r)

    line = iota((head_rows, slots), 0)
    row_slot = slot_of(line // (2 * ROWS_DEV) * TILE + line % ROWS_DEV, nx)
    row_pick = (row_slot == iota((head_rows, slots), 1)).astype(BF16)
    first_map = (iota((head_rows, 1), 0) // ROWS_DEV) % 2 == 0
    low = iota((slots, slots), 0)
    high = iota((slots, slots), 1)
    trees = []
    for r in range(nr):
        link = (low == parents[r : r + 1, :]) & (high >= 1)
        trees.append((link | (low == high)).astype(F32).astype(BF16))
    for _ in range(max(1, (slots - 1).bit_length())):
        trees = [jnp.minimum(jnp.dot(t, t, preferred_element_type=F32), 1.0).astype(BF16) for t in trees]
    for r in range(nr):
        tree[r] = trees[r]
        depth = jnp.sum(nt(row_pick, trees[r]), axis=1, keepdims=True) - 1.0
        oldest[r] = depth + (lengths[r] - window).astype(F32)

    arrived(q_all)
    q_c = gather_core(gq, qc_s, qc_r)
    arrived(kv_z)
    kv_x = gather_x(gkv, kx_s, kx_r)
    arrived(q_c)

    scale = LOG2E / math.sqrt(QK)
    position = (seq * span + iota((1, span), 1)).astype(F32)

    def attend(k):
        r = order[k]
        q = gq[:, :, pl.ds(2 * r, 2)].reshape(rows, QK).astype(F32).reshape(rows // TILE, 2, 2 * ROWS_DEV, QK)
        reach = jnp.where(position < SINKS, -FILL_LOW, position)
        reach = jnp.where(position < lengths[r].astype(F32), reach, FILL_LOW)
        allowed = reach > oldest[r]
        bodies, stats = [], []
        for h in range(2):
            mine = q[:, h].reshape(head_rows, QK)
            wide = jnp.concatenate([jnp.where(first_map, mine, 0.0), jnp.where(first_map, 0.0, mine)], axis=1).astype(BF16)
            scores = jnp.where(allowed, nt(wide, kc[r, h]) * scale, FILL_LOW)
            shift = jnp.max(scores, axis=1, keepdims=True).astype(BF16).astype(F32)
            weight = jnp.where(allowed, jnp.exp2(scores - shift), 0.0)
            total = jnp.sum(weight, axis=1, keepdims=True)
            bodies.append(jnp.dot(weight.astype(BF16), vc[r, h], preferred_element_type=F32))
            stats.append(stat_lanes(shift, total))

        def weave(pair):
            width = pair[0].shape[1]
            pair = [p.reshape(rows // TILE, 1, 2 * ROWS_DEV, width) for p in pair]
            return jnp.concatenate(pair, axis=1).reshape(rows, width).astype(BF16).reshape(NC, nx, 2, TILE, width)

        part[k, :, :, :, :, :VD] = weave(bodies)
        part[k, :, :, :, :, VD:] = weave(stats)
        copy = remote(part.at[k, other], core_in.at[k], rc_s.at[k], rc_r.at[k], device(z, x, other))
        copy.start()
        sent.append(copy)
        return copy

    def chip_merge(k, copy):
        copy.wait_recv()
        block = nx * 2 * TILE
        mine = part[k, core].reshape(block, MSG)
        theirs = core_in[k].reshape(block, MSG)
        body, stats = pack(merge([unpack(mine), unpack(theirs)]))
        chip[k, :, :, :, :VD] = body.reshape(nx, 2, TILE, VD)
        chip[k, :, :, :, VD:] = stats.reshape(nx, 2, TILE, 128)

    def send_x(k):
        waits = []
        for d, to, source in x_peers:
            copy = remote(chip.at[k, to], x_in.at[k, d], rx_s.at[k, d], rx_r.at[k, d], device(z, to, core))
            copy.start()
            sent.append(copy)
            waits.append(copy)
        return waits

    def to_owner(src, k, zl, d, zz, xx):
        copy = remote(src, z_in.at[z, x], rz_s.at[k, zl, d], rz_r.at[z, x], device(zz, xx, core))
        copy.start()
        sent.append(copy)

    def plane_merge(k, waits):
        arrived(waits)
        parts = [unpack(chip[k, x].reshape(2 * TILE, MSG))]
        for d, _, _ in x_peers:
            parts.append(unpack(x_in[k, d].reshape(2 * TILE, MSG)))
        body, stats = pack(merge(parts))
        plane[k, :, :, :VD] = body.reshape(2, TILE, VD)
        plane[k, :, :, VD:] = stats.reshape(2, TILE, 128)
        if k == last:
            to_owner(plane.at[k, 1 - z % 2], k, 0, 0, z + 2 * even - 1, x)
            z_in[z, x] = plane[k, z % 2]
            return
        for zl in range(2):
            to_owner(plane.at[k, zl], k, zl, 0, 2 * order[k] + zl, x)

    def send_direct(k):
        if k < last:
            for d in range(nx - 1, -1, -1):
                for zl in range(2):
                    xx = (x + d) % nx
                    to_owner(chip.at[k, xx, zl], k, zl, d, 2 * order[k] + zl, xx)
            return
        mate = z + 2 * even - 1
        for d in range(nx - 1, -1, -1):
            xx = (x + d) % nx
            to_owner(chip.at[k, xx, mate % 2], k, 0, d, mate, xx)
            if d > 0:
                to_owner(chip.at[k, xx, z % 2], k, 1, d, z, xx)
        z_in[z, x] = chip[k, x, z % 2]

    for pair in loads:
        for copy in pair:
            copy.wait()
    in_core, in_x = {}, {}

    def spread(k):
        chip_merge(k, in_core[k])
        if k in STAGED:
            in_x[k] = send_x(k)
        else:
            send_direct(k)

    def settle(k):
        if k in STAGED:
            plane_merge(k, in_x[k])

    in_core[0] = attend(0)
    in_core[1] = attend(1)
    spread(0)
    in_core[2] = attend(2)
    spread(1)
    in_core[3] = attend(3)
    arrived(kv_x)
    kv_c = gather_core(gkv, kc_s, kc_r)
    spread(2)
    settle(0)
    spread(3)
    settle(1)
    settle(2)
    arrived(kv_c)
    row_chunk_lane = chunk_of(iota((slots, rows), 1))
    slot_lane = slot_of(iota((slots, rows), 1), nx)

    def write(r):
        begin = lengths[r] - seq * span
        taken = (iota((span, slots), 0) - begin == iota((span, slots), 1)) & (iota((span, slots), 1) < accepted[r])
        taken = taken.astype(BF16)
        place = iota((span, 1), 0) - begin
        touched = (place >= 0) & (place < accepted[r])
        slot_order = (path[r : r + 1, :] == iota((slots, slots), 0)).astype(BF16)
        lanes = (slot_lane == iota((slots, rows), 0)).astype(BF16)
        wide = lax.dot_general(slot_order, lanes, (((0,), (0,)), ((), ())), preferred_element_type=F32)
        for i, buf in enumerate((kc, vc)):
            block = gkv[:, :, 2 * r : 2 * r + 2, i].reshape(rows, 128)
            for h in range(2):
                kept = [
                    jnp.dot(
                        jnp.where(row_chunk_lane == 2 * h + half, wide, 0.0).astype(BF16), block, preferred_element_type=F32
                    ).astype(BF16)
                    for half in range(2)
                ]
                fresh = jnp.dot(taken, jnp.concatenate(kept, axis=1), preferred_element_type=F32)
                buf[r, h] = jnp.where(touched, fresh, buf[r, h].astype(F32)).astype(BF16)


    own_slot = ((z % 2) * nx + x) * NC + core
    own_slot = own_slot * ROWS_DEV
    keys_own = gkv[:, :, pl.ds(2 * own, 2), 0].reshape(rows, QK)
    values_own = gkv[:, :, pl.ds(2 * own, 2), 1].reshape(rows, QK)
    pick_row = (own_slot + iota((TILE, slots), 0) % ROWS_DEV == iota((TILE, slots), 1)).astype(BF16)
    live = (iota((TILE, slots), 1) < draft_counts[own]).astype(F32)
    seen = (nt(pick_row, tree[own]) * live).astype(BF16)
    pick_lane = (slot_of(iota((slots, rows), 1), nx) == iota((slots, rows), 0)).astype(BF16)
    lane_chunk = chunk_of(iota((TILE, rows), 1))
    row_chunk = iota((TILE, rows), 0) // ROWS_DEV
    allowed = (jnp.dot(seen, pick_lane, preferred_element_type=F32) > 0.5) & (lane_chunk == row_chunk)
    scores = jnp.where(allowed, nt(gq[core, x, z], keys_own) * scale, FILL_LOW)
    shift = jnp.max(scores, axis=1, keepdims=True)
    weight = jnp.where(allowed, jnp.exp2(scores - shift), 0.0)
    total = jnp.sum(weight, axis=1, keepdims=True)
    even_chunk = row_chunk % 2 == 0
    ahead = pltpu.roll(weight, ROWS_DEV, 1)
    behind = pltpu.roll(weight, rows - ROWS_DEV, 1)
    left = jnp.where(even_chunk, weight, behind).astype(BF16)
    right = jnp.where(even_chunk, ahead, weight).astype(BF16)
    weighted = jnp.concatenate(
        [
            jnp.dot(left, values_own, preferred_element_type=F32),
            jnp.dot(right, values_own, preferred_element_type=F32),
        ],
        axis=1,
    )
    draft = (shift, total, weighted)

    parts = [draft, unpack(z_in[z, x])]

    def take(zz, xx):
        remote(plane.at[0, 0], z_in.at[zz, xx], rz_s.at[0, 0, 0], rz_r.at[zz, xx], device(zz, xx, core)).wait_recv()
        parts.append(unpack(z_in[zz, xx]))

    for d in range(nx):
        if last not in STAGED:
            take(z + 2 * even - 1, (x + d) % nx)
            if d > 0:
                take(z, (x + d) % nx)
        elif d == 0:
            take(z + 2 * even - 1, x)
    parts = [merge(parts)]
    for step in range(2, nz):
        source = (2 * own + step) % nz
        rank = {nz // 2: 0, nz // 2 + 1: 0, nz // 2 - 1: 1, nz - 2: 1}.get(step, 2)
        if rank in STAGED:
            take(source, x)
        else:
            for xx in range(nx):
                take(source, xx)
    peak, total, weighted = merge(parts)
    attended = weighted / total
    row_live = own_slot + iota((ROWS_DEV, 1), 0) < draft_counts[own]
    normed = []
    for h in range(2):
        first = attended[2 * h * ROWS_DEV : (2 * h + 1) * ROWS_DEV]
        second = attended[(2 * h + 1) * ROWS_DEV : (2 * h + 2) * ROWS_DEV]
        difference = first - lambdas[h] * second
        square = jnp.mean(difference * difference, axis=1, keepdims=True)
        scaled = difference * lax.rsqrt(square + EPSILON) * gain[...] * OUT_SCALE
        normed.append(jnp.where(row_live, scaled, 0.0).astype(BF16))
    load_w.wait()
    product = jnp.dot(jnp.concatenate(normed, axis=1), wv[...], preferred_element_type=F32)
    width = mixed.shape[1]
    for h in range(nh):
        y_out[h] = product[:, h * width : (h + 1) * width]
    waits = []
    for d, to, source in h_peers:
        copy = remote(y_out.at[to], y_in.at[d], y_s.at[d], y_r.at[d], (seq, to))
        copy.start()
        sent.append(copy)
        waits.append(copy)
    for r in range(nr):
        write(r)
    for copy in sent[: -len(waits)] if waits else sent:
        copy.wait_send()
    summed = y_out[head]
    arrived(waits)
    for d, _, _ in h_peers:
        summed = summed + y_in[d]
    mixed[...] = (summed + hidden[...].astype(F32)).astype(BF16)

    for copy in waits:
        copy.wait_send()


def store_kernel(nr, mixed_in, kc, vc, mixed, new_k, new_v, sem):
    copies = []
    for r in range(nr):
        copies.append(pltpu.make_async_copy(kc.at[r], new_k.at[r], sem.at[2 * r]))
        copies.append(pltpu.make_async_copy(vc.at[r], new_v.at[r], sem.at[2 * r + 1]))
    copies.append(pltpu.make_async_copy(mixed_in, mixed, sem.at[2 * nr]))
    for copy in copies:
        copy.start()
    for copy in copies:
        copy.wait()


def body(
    nz, nx, nh, window,
    hidden, draft_queries, draft_keys, draft_values, cache_k, cache_v, lambdas, norm_gain, out_weight,
    lengths, parents, draft_counts, accepted_path, accepted_count,
):
    nr = nz // 2
    slots = 2 * nx * NC * ROWS_DEV
    rows = 2 * nx * NC * TILE
    vmem = pl.BlockSpec(memory_space=pltpu.VMEM)
    hbm = pl.BlockSpec(memory_space=pltpu.MemorySpace.HBM)
    dma = pltpu.SemaphoreType.DMA
    kv_shape = (NC, nx, nz, 2, TILE, 128)
    to_hbm = [
        pltpu.with_memory_space_constraint(a, pltpu.MemorySpace.HBM)
        for a in (
            lengths, draft_counts, lambdas, hidden, draft_queries, draft_keys, draft_values,
            norm_gain.reshape(1, VD), parents, accepted_path, accepted_count, cache_k, cache_v, out_weight,
        )
    ]
    mixed, kc, vc = pl.pallas_call(
        functools.partial(attention_kernel, nz, nx, nh, window),
        out_shape=(pltpu.VMEM(hidden.shape, BF16), pltpu.VMEM(cache_k.shape, BF16), pltpu.VMEM(cache_v.shape, BF16)),
        in_specs=[hbm] * 14,
        out_specs=(vmem, vmem, vmem),
        scratch_shapes=[
            pltpu.VMEM(accepted_path.shape, I32),
            pltpu.SMEM(accepted_count.shape, I32),
            pltpu.SMEM(lengths.shape, I32),
            pltpu.SMEM(draft_counts.shape, I32),
            pltpu.SMEM(lambdas.shape, F32),
            pltpu.VMEM(hidden.shape, BF16),
            pltpu.VMEM(hidden.shape, BF16),
            pltpu.VMEM(hidden.shape, BF16),
            pltpu.VMEM(hidden.shape, BF16),
            pltpu.VMEM((1, VD), F32),
            pltpu.VMEM(parents.shape, I32),
            pltpu.VMEM((NC, nx, nz, TILE, 128), BF16),
            pltpu.VMEM(kv_shape, BF16),
            pltpu.VMEM(out_weight.shape, BF16),
            pltpu.VMEM((nr, slots, slots), BF16),
            pltpu.VMEM((nr, rows // 2, 1), F32),
            pltpu.VMEM((nr, NC, nx, 2, TILE, MSG), BF16),
            pltpu.VMEM((nr, nx, 2, TILE, MSG), BF16),
            pltpu.VMEM((nr, nx, 2, TILE, MSG), BF16),
            pltpu.VMEM((nr, nx, 2, TILE, MSG), BF16),
            pltpu.VMEM((nr, 2, TILE, MSG), BF16),
            pltpu.VMEM((nz, nx, TILE, MSG), BF16),
            pltpu.VMEM((nh, ROWS_DEV, hidden.shape[1]), F32),
            pltpu.VMEM((nh, ROWS_DEV, hidden.shape[1]), F32),
            dma((nz, nx)), dma((nz, nx)), dma((nx,)), dma((nx,)), dma, dma,
            dma((nz,)), dma((nz,)), dma((nx,)), dma((nx,)), dma, dma,
            dma((nr,)), dma((nr,)), dma((nr, nx)), dma((nr, nx)), dma((nr, 2, nx)), dma((nz, nx)), dma((nh,)), dma((nh,)),
            dma((nr, 2)), dma, dma((11,)),
        ],
        compiler_params=pltpu.CompilerParams(collective_id=0, has_side_effects=True, vmem_limit_bytes=48 << 20),
    )(*to_hbm)
    return pl.pallas_call(
        functools.partial(store_kernel, nr),
        out_shape=(
            jax.ShapeDtypeStruct(hidden.shape, BF16),
            jax.ShapeDtypeStruct(cache_k.shape, BF16),
            jax.ShapeDtypeStruct(cache_v.shape, BF16),
        ),
        in_specs=[vmem] * 3,
        out_specs=(hbm, hbm, hbm),
        scratch_shapes=[dma((2 * nr + 1,))],
        compiler_params=pltpu.CompilerParams(vmem_limit_bytes=2 << 20),
    )(*[pltpu.with_memory_space_constraint(a, pltpu.MemorySpace.VMEM) for a in (mixed, kc, vc)])


def build(mesh, nz, nx, window):
    seq_rows = P("seq", "head")
    cache = P(None, "head", "seq", None)
    in_specs = (seq_rows,) * 4 + (cache, cache, P("head"), P(), P("head", None)) + (P(),) * 5
    return jax.shard_map(
        functools.partial(body, nz, nx, mesh.shape["head"], window),
        mesh=mesh,
        in_specs=in_specs,
        out_specs=(seq_rows, cache, cache),
        check_vma=False,
    )


def solution(mesh):
    return build(mesh, 8, 4, 4096)
```

```python
import functools
import math

import jax
import jax.numpy as jnp
from jax import lax
from jax.experimental import pallas as pl
from jax.experimental.pallas import tpu as pltpu
from jax.sharding import PartitionSpec as P

MESH = pl.DeviceIdType.MESH
F32 = jnp.float32
BF16 = jnp.bfloat16
I32 = jnp.int32

SINKS = 4
FILL_LOW = -1e30
EPSILON = 1e-05
OUT_SCALE = 0.8
LOG2E = 1.4426950408889634

STAGED = (0, 1)
NC = 2
ROWS_DEV = 4
CHUNKS = 4
TILE = ROWS_DEV * CHUNKS
QK = 128
VD = 256
MSG = VD + 128


def nt(a, b):
    return lax.dot_general(a, b, (((1,), (1,)), ((), ())), preferred_element_type=F32)


def iota(shape, dim):
    return lax.broadcasted_iota(I32, shape, dim)


def slot_of(index, nx):
    row = index % ROWS_DEV
    zl = (index // TILE) % 2
    x = (index // (2 * TILE)) % nx
    core = index // (2 * TILE * nx)
    return ((zl * nx + x) * NC + core) * ROWS_DEV + row


def chunk_of(index):
    return (index // ROWS_DEV) % CHUNKS


def tile_of(ref):
    value = ref[...].astype(F32)
    pieces = [value[:, QK * c : QK * (c + 1)] for c in range(CHUNKS)]
    return jnp.concatenate(pieces, axis=0).astype(BF16)


def unpack(message):
    wide = message.astype(F32)
    shift = wide[:, VD : VD + 1]
    total = wide[:, VD + 1 : VD + 2] + wide[:, VD + 2 : VD + 3]
    return shift, total, wide[:, :VD]


def merge(parts):
    peak = functools.reduce(jnp.maximum, [p[0] for p in parts])
    factors = [jnp.exp2(p[0] - peak) for p in parts]
    total = sum(f * p[1] for f, p in zip(factors, parts))
    weighted = sum(f * p[2] for f, p in zip(factors, parts))
    return peak, total, weighted


def stat_lanes(shift, total):
    high = total.astype(BF16).astype(F32)
    lane = iota((shift.shape[0], 128), 1)
    return jnp.where(lane == 0, shift, jnp.where(lane == 1, high, total - high))


def pack(part):
    shift, total, weighted = part
    return weighted.astype(BF16), stat_lanes(shift, total).astype(BF16)


def attention_kernel(
    nz, nx, nh, window,
    lengths_in, draft_counts_in, lambdas_in, hidden_in, queries_in, keys_in, values_in, gain_in, parents_in,
    path_in, accepted_in, cache_k, cache_v, out_weight,
    mixed, kc, vc,
    path, accepted, lengths, draft_counts, lambdas, hidden, queries, keys, values, gain, parents,
    gq, gkv, wv, tree, oldest, part, core_in, chip, x_in, plane, z_in, y_out, y_in,
    qz_s, qz_r, qx_s, qx_r, qc_s, qc_r, kz_s, kz_r, kx_s, kx_r, kc_s, kc_r,
    rc_s, rc_r, rx_s, rx_r, rz_s, rz_r, y_s, y_r, load_sem, w_sem, small_sem,
):
    nr = nz // 2
    slots = 2 * nx * NC * ROWS_DEV
    span = cache_k.shape[2]
    rows = 2 * nx * NC * TILE
    head_rows = rows // 2
    seq = lax.axis_index("seq")
    head = lax.axis_index("head")
    core = seq % NC
    x = (seq // NC) % nx
    z = seq // (NC * nx)

    def device(zz, xx, cc):
        return ((zz * nx + xx) * NC + cc, head)

    def remote(src, dst, send, recv, target):
        return pltpu.make_async_remote_copy(
            src_ref=src, dst_ref=dst, send_sem=send, recv_sem=recv, device_id=target, device_id_type=MESH
        )

    z_peers = [(d, (z + d) % nz, (z + nz - d) % nz) for d in range(1, nz)]
    x_peers = [(d, (x + d) % nx, (x + nx - d) % nx) for d in range(1, nx)]
    h_peers = [(d, (head + d) % nh, (head + nh - d) % nh) for d in range(1, nh)]
    other = 1 - core
    own = z // 2
    even = 1 - z % 2
    order = [(own + nr // 2) % nr, (own + nr - 1 + 2 * even) % nr, (own + nr + 1 - 2 * even) % nr, own]
    last = len(order) - 1

    small = [
        pltpu.make_async_copy(src, dst, small_sem.at[i])
        for i, (src, dst) in enumerate(
            [
                (queries_in, queries), (keys_in, keys), (values_in, values), (parents_in, parents), (lengths_in, lengths),
                (path_in, path), (accepted_in, accepted), (draft_counts_in, draft_counts), (lambdas_in, lambdas), (hidden_in, hidden), (gain_in, gain),
            ]
        )
    ]
    small[0].start()
    barrier = pltpu.get_barrier_semaphore()
    peers = [device(z, x, other)]
    peers += [device(to, x, core) for _, to, _ in z_peers]
    peers += [device(z, to, core) for _, to, _ in x_peers]
    peers += [device((z + dz) % nz, (x + dx) % nx, core) for dz in range(1, nz) for dx in range(1, nx)]
    peers += [(seq, to) for _, to, _ in h_peers]
    for peer in peers:
        pl.semaphore_signal(barrier, inc=1, device_id=peer, device_id_type=MESH)

    loads = []
    for r in range(nr):
        loads.append(
            (
                pltpu.make_async_copy(cache_k.at[r], kc.at[r], load_sem.at[r, 0]),
                pltpu.make_async_copy(cache_v.at[r], vc.at[r], load_sem.at[r, 1]),
            )
        )
    load_w = pltpu.make_async_copy(out_weight, wv, w_sem)
    for copy in small[1:]:
        copy.start()
    small[0].wait()
    gq[core, x, z] = tile_of(queries)

    pl.semaphore_wait(barrier, len(peers))

    sent = []

    def gather_z(buf, send, recv):
        waits = []
        for d, to, source in z_peers:
            copy = remote(buf.at[core, x, z], buf.at[core, x, z], send.at[d], recv.at[d], device(to, x, core))
            copy.start()
            sent.append(copy)
            waits.append(remote(buf.at[core, x, z], buf.at[core, x, source], send.at[d], recv.at[d], device(to, x, core)))
        return waits

    def gather_x(buf, send, recv):
        waits = []
        for d, to, source in x_peers:
            copy = remote(buf.at[core, x], buf.at[core, x], send.at[d], recv.at[d], device(z, to, core))
            copy.start()
            sent.append(copy)
            waits.append(remote(buf.at[core, x], buf.at[core, source], send.at[d], recv.at[d], device(z, to, core)))
        return waits

    def gather_core(buf, send, recv):
        copy = remote(buf.at[core], buf.at[core], send, recv, device(z, x, other))
        copy.start()
        sent.append(copy)
        return [remote(buf.at[core], buf.at[other], send, recv, device(z, x, other))]

    def arrived(waits):
        for copy in waits:
            copy.wait_recv()

    q_all = []
    for dz in sorted(range(nz), key=lambda i: -min(i, nz - i)):
        for dx in sorted(range(nx), key=lambda i: -min(i, nx - i)):
            if dz + dx > 0:
                mine = gq.at[core, x, z]
                target = device((z + dz) % nz, (x + dx) % nx, core)
                copy = remote(mine, mine, qz_s.at[dz, dx], qz_r.at[dz, dx], target)
                copy.start()
                sent.append(copy)
                theirs = gq.at[core, (x + nx - dx) % nx, (z + nz - dz) % nz]
                q_all.append(remote(mine, theirs, qz_s.at[dz, dx], qz_r.at[dz, dx], target))
    for copy_k, copy_v in loads:
        copy_k.start()
        copy_v.start()
    load_w.start()
    for copy in small[1:]:
        copy.wait()
    gkv[core, x, z, 0] = tile_of(keys)
    gkv[core, x, z, 1] = tile_of(values)
    kv_z = gather_z(gkv, kz_s, kz_r)

    line = iota((head_rows, slots), 0)
    row_slot = slot_of(line // (2 * ROWS_DEV) * TILE + line % ROWS_DEV, nx)
    row_pick = (row_slot == iota((head_rows, slots), 1)).astype(BF16)
    first_map = (iota((head_rows, 1), 0) // ROWS_DEV) % 2 == 0
    low = iota((slots, slots), 0)
    high = iota((slots, slots), 1)
    trees = []
    for r in range(nr):
        link = (low == parents[r : r + 1, :]) & (high >= 1)
        trees.append((link | (low == high)).astype(F32).astype(BF16))
    for _ in range(max(1, (slots - 1).bit_length())):
        trees = [jnp.minimum(jnp.dot(t, t, preferred_element_type=F32), 1.0).astype(BF16) for t in trees]
    for r in range(nr):
        tree[r] = trees[r]
        depth = jnp.sum(nt(row_pick, trees[r]), axis=1, keepdims=True) - 1.0
        oldest[r] = depth + (lengths[r] - window).astype(F32)

    arrived(q_all)
    q_c = gather_core(gq, qc_s, qc_r)
    arrived(kv_z)
    kv_x = gather_x(gkv, kx_s, kx_r)
    arrived(q_c)

    scale = LOG2E / math.sqrt(QK)
    position = (seq * span + iota((1, span), 1)).astype(F32)

    def attend(k):
        r = order[k]
        q = gq[:, :, pl.ds(2 * r, 2)].reshape(rows, QK).astype(F32).reshape(rows // TILE, 2, 2 * ROWS_DEV, QK)
        reach = jnp.where(position < SINKS, -FILL_LOW, position)
        reach = jnp.where(position < lengths[r].astype(F32), reach, FILL_LOW)
        allowed = reach > oldest[r]
        bodies, stats = [], []
        for h in range(2):
            mine = q[:, h].reshape(head_rows, QK)
            wide = jnp.concatenate([jnp.where(first_map, mine, 0.0), jnp.where(first_map, 0.0, mine)], axis=1).astype(BF16)
            scores = jnp.where(allowed, nt(wide, kc[r, h]) * scale, FILL_LOW)
            shift = jnp.max(scores, axis=1, keepdims=True).astype(BF16).astype(F32)
            weight = jnp.where(allowed, jnp.exp2(scores - shift), 0.0)
            total = jnp.sum(weight, axis=1, keepdims=True)
            bodies.append(jnp.dot(weight.astype(BF16), vc[r, h], preferred_element_type=F32))
            stats.append(stat_lanes(shift, total))

        def weave(pair):
            width = pair[0].shape[1]
            pair = [p.reshape(rows // TILE, 1, 2 * ROWS_DEV, width) for p in pair]
            return jnp.concatenate(pair, axis=1).reshape(rows, width).astype(BF16).reshape(NC, nx, 2, TILE, width)

        part[k, :, :, :, :, :VD] = weave(bodies)
        part[k, :, :, :, :, VD:] = weave(stats)
        copy = remote(part.at[k, other], core_in.at[k], rc_s.at[k], rc_r.at[k], device(z, x, other))
        copy.start()
        sent.append(copy)
        return copy

    def chip_merge(k, copy):
        copy.wait_recv()
        block = nx * 2 * TILE
        mine = part[k, core].reshape(block, MSG)
        theirs = core_in[k].reshape(block, MSG)
        body, stats = pack(merge([unpack(mine), unpack(theirs)]))
        chip[k, :, :, :, :VD] = body.reshape(nx, 2, TILE, VD)
        chip[k, :, :, :, VD:] = stats.reshape(nx, 2, TILE, 128)

    def send_x(k):
        waits = []
        for d, to, source in x_peers:
            copy = remote(chip.at[k, to], x_in.at[k, d], rx_s.at[k, d], rx_r.at[k, d], device(z, to, core))
            copy.start()
            sent.append(copy)
            waits.append(copy)
        return waits

    def to_owner(src, k, zl, d, zz, xx):
        copy = remote(src, z_in.at[z, x], rz_s.at[k, zl, d], rz_r.at[z, x], device(zz, xx, core))
        copy.start()
        sent.append(copy)

    def plane_merge(k, waits):
        arrived(waits)
        parts = [unpack(chip[k, x].reshape(2 * TILE, MSG))]
        for d, _, _ in x_peers:
            parts.append(unpack(x_in[k, d].reshape(2 * TILE, MSG)))
        body, stats = pack(merge(parts))
        plane[k, :, :, :VD] = body.reshape(2, TILE, VD)
        plane[k, :, :, VD:] = stats.reshape(2, TILE, 128)
        if k == last:
            to_owner(plane.at[k, 1 - z % 2], k, 0, 0, z + 2 * even - 1, x)
            z_in[z, x] = plane[k, z % 2]
            return
        for zl in range(2):
            to_owner(plane.at[k, zl], k, zl, 0, 2 * order[k] + zl, x)

    def send_direct(k):
        if k < last:
            for d in range(nx - 1, -1, -1):
                for zl in range(2):
                    xx = (x + d) % nx
                    to_owner(chip.at[k, xx, zl], k, zl, d, 2 * order[k] + zl, xx)
            return
        mate = z + 2 * even - 1
        for d in range(nx - 1, -1, -1):
            xx = (x + d) % nx
            to_owner(chip.at[k, xx, mate % 2], k, 0, d, mate, xx)
            if d > 0:
                to_owner(chip.at[k, xx, z % 2], k, 1, d, z, xx)
        z_in[z, x] = chip[k, x, z % 2]

    for pair in loads:
        for copy in pair:
            copy.wait()
    in_core, in_x = {}, {}

    def spread(k):
        chip_merge(k, in_core[k])
        if k in STAGED:
            in_x[k] = send_x(k)
        else:
            send_direct(k)

    def settle(k):
        if k in STAGED:
            plane_merge(k, in_x[k])

    in_core[0] = attend(0)
    in_core[1] = attend(1)
    spread(0)
    in_core[2] = attend(2)
    spread(1)
    in_core[3] = attend(3)
    arrived(kv_x)
    kv_c = gather_core(gkv, kc_s, kc_r)
    spread(2)
    settle(0)
    spread(3)
    settle(1)
    settle(2)
    arrived(kv_c)
    row_chunk_lane = chunk_of(iota((slots, rows), 1))
    slot_lane = slot_of(iota((slots, rows), 1), nx)

    def write(r):
        begin = lengths[r] - seq * span
        taken = (iota((span, slots), 0) - begin == iota((span, slots), 1)) & (iota((span, slots), 1) < accepted[r])
        taken = taken.astype(BF16)
        place = iota((span, 1), 0) - begin
        touched = (place >= 0) & (place < accepted[r])
        slot_order = (path[r : r + 1, :] == iota((slots, slots), 0)).astype(BF16)
        lanes = (slot_lane == iota((slots, rows), 0)).astype(BF16)
        wide = lax.dot_general(slot_order, lanes, (((0,), (0,)), ((), ())), preferred_element_type=F32)
        for i, buf in enumerate((kc, vc)):
            block = gkv[:, :, 2 * r : 2 * r + 2, i].reshape(rows, 128)
            for h in range(2):
                kept = [
                    jnp.dot(
                        jnp.where(row_chunk_lane == 2 * h + half, wide, 0.0).astype(BF16), block, preferred_element_type=F32
                    ).astype(BF16)
                    for half in range(2)
                ]
                fresh = jnp.dot(taken, jnp.concatenate(kept, axis=1), preferred_element_type=F32)
                buf[r, h] = jnp.where(touched, fresh, buf[r, h].astype(F32)).astype(BF16)


    for r in range(nr - 1):
        write(r)

    own_slot = ((z % 2) * nx + x) * NC + core
    own_slot = own_slot * ROWS_DEV
    keys_own = gkv[:, :, pl.ds(2 * own, 2), 0].reshape(rows, QK)
    values_own = gkv[:, :, pl.ds(2 * own, 2), 1].reshape(rows, QK)
    pick_row = (own_slot + iota((TILE, slots), 0) % ROWS_DEV == iota((TILE, slots), 1)).astype(BF16)
    live = (iota((TILE, slots), 1) < draft_counts[own]).astype(F32)
    seen = (nt(pick_row, tree[own]) * live).astype(BF16)
    pick_lane = (slot_of(iota((slots, rows), 1), nx) == iota((slots, rows), 0)).astype(BF16)
    lane_chunk = chunk_of(iota((TILE, rows), 1))
    row_chunk = iota((TILE, rows), 0) // ROWS_DEV
    allowed = (jnp.dot(seen, pick_lane, preferred_element_type=F32) > 0.5) & (lane_chunk == row_chunk)
    scores = jnp.where(allowed, nt(gq[core, x, z], keys_own) * scale, FILL_LOW)
    shift = jnp.max(scores, axis=1, keepdims=True)
    weight = jnp.where(allowed, jnp.exp2(scores - shift), 0.0)
    total = jnp.sum(weight, axis=1, keepdims=True)
    even_chunk = row_chunk % 2 == 0
    ahead = pltpu.roll(weight, ROWS_DEV, 1)
    behind = pltpu.roll(weight, rows - ROWS_DEV, 1)
    left = jnp.where(even_chunk, weight, behind).astype(BF16)
    right = jnp.where(even_chunk, ahead, weight).astype(BF16)
    weighted = jnp.concatenate(
        [
            jnp.dot(left, values_own, preferred_element_type=F32),
            jnp.dot(right, values_own, preferred_element_type=F32),
        ],
        axis=1,
    )
    draft = (shift, total, weighted)

    parts = [draft, unpack(z_in[z, x])]

    def take(zz, xx):
        remote(plane.at[0, 0], z_in.at[zz, xx], rz_s.at[0, 0, 0], rz_r.at[zz, xx], device(zz, xx, core)).wait_recv()
        parts.append(unpack(z_in[zz, xx]))

    for d in range(nx):
        if last not in STAGED:
            take(z + 2 * even - 1, (x + d) % nx)
            if d > 0:
                take(z, (x + d) % nx)
        elif d == 0:
            take(z + 2 * even - 1, x)
    parts = [merge(parts)]
    for step in range(2, nz):
        source = (2 * own + step) % nz
        rank = {nz // 2: 0, nz // 2 + 1: 0, nz // 2 - 1: 1, nz - 2: 1}.get(step, 2)
        if rank in STAGED:
            take(source, x)
        else:
            for xx in range(nx):
                take(source, xx)
    peak, total, weighted = merge(parts)
    attended = weighted / total
    row_live = own_slot + iota((ROWS_DEV, 1), 0) < draft_counts[own]
    normed = []
    for h in range(2):
        first = attended[2 * h * ROWS_DEV : (2 * h + 1) * ROWS_DEV]
        second = attended[(2 * h + 1) * ROWS_DEV : (2 * h + 2) * ROWS_DEV]
        difference = first - lambdas[h] * second
        square = jnp.mean(difference * difference, axis=1, keepdims=True)
        scaled = difference * lax.rsqrt(square + EPSILON) * gain[...] * OUT_SCALE
        normed.append(jnp.where(row_live, scaled, 0.0).astype(BF16))
    load_w.wait()
    product = jnp.dot(jnp.concatenate(normed, axis=1), wv[...], preferred_element_type=F32)
    width = mixed.shape[1]
    for h in range(nh):
        y_out[h] = product[:, h * width : (h + 1) * width]
    waits = []
    for d, to, source in h_peers:
        copy = remote(y_out.at[to], y_in.at[d], y_s.at[d], y_r.at[d], (seq, to))
        copy.start()
        sent.append(copy)
        waits.append(copy)
    for r in range(nr - 1, nr):
        write(r)
    for copy in sent[: -len(waits)] if waits else sent:
        copy.wait_send()
    summed = y_out[head]
    arrived(waits)
    for d, _, _ in h_peers:
        summed = summed + y_in[d]
    mixed[...] = (summed + hidden[...].astype(F32)).astype(BF16)

    for copy in waits:
        copy.wait_send()


def store_kernel(nr, mixed_in, kc, vc, mixed, new_k, new_v, sem):
    copies = []
    for r in range(nr):
        copies.append(pltpu.make_async_copy(kc.at[r], new_k.at[r], sem.at[2 * r]))
        copies.append(pltpu.make_async_copy(vc.at[r], new_v.at[r], sem.at[2 * r + 1]))
    copies.append(pltpu.make_async_copy(mixed_in, mixed, sem.at[2 * nr]))
    for copy in copies:
        copy.start()
    for copy in copies:
        copy.wait()


def body(
    nz, nx, nh, window,
    hidden, draft_queries, draft_keys, draft_values, cache_k, cache_v, lambdas, norm_gain, out_weight,
    lengths, parents, draft_counts, accepted_path, accepted_count,
):
    nr = nz // 2
    slots = 2 * nx * NC * ROWS_DEV
    rows = 2 * nx * NC * TILE
    vmem = pl.BlockSpec(memory_space=pltpu.VMEM)
    hbm = pl.BlockSpec(memory_space=pltpu.MemorySpace.HBM)
    dma = pltpu.SemaphoreType.DMA
    kv_shape = (NC, nx, nz, 2, TILE, 128)
    to_hbm = [
        pltpu.with_memory_space_constraint(a, pltpu.MemorySpace.HBM)
        for a in (
            lengths, draft_counts, lambdas, hidden, draft_queries, draft_keys, draft_values,
            norm_gain.reshape(1, VD), parents, accepted_path, accepted_count, cache_k, cache_v, out_weight,
        )
    ]
    mixed, kc, vc = pl.pallas_call(
        functools.partial(attention_kernel, nz, nx, nh, window),
        out_shape=(pltpu.VMEM(hidden.shape, BF16), pltpu.VMEM(cache_k.shape, BF16), pltpu.VMEM(cache_v.shape, BF16)),
        in_specs=[hbm] * 14,
        out_specs=(vmem, vmem, vmem),
        scratch_shapes=[
            pltpu.VMEM(accepted_path.shape, I32),
            pltpu.SMEM(accepted_count.shape, I32),
            pltpu.SMEM(lengths.shape, I32),
            pltpu.SMEM(draft_counts.shape, I32),
            pltpu.SMEM(lambdas.shape, F32),
            pltpu.VMEM(hidden.shape, BF16),
            pltpu.VMEM(hidden.shape, BF16),
            pltpu.VMEM(hidden.shape, BF16),
            pltpu.VMEM(hidden.shape, BF16),
            pltpu.VMEM((1, VD), F32),
            pltpu.VMEM(parents.shape, I32),
            pltpu.VMEM((NC, nx, nz, TILE, 128), BF16),
            pltpu.VMEM(kv_shape, BF16),
            pltpu.VMEM(out_weight.shape, BF16),
            pltpu.VMEM((nr, slots, slots), BF16),
            pltpu.VMEM((nr, rows // 2, 1), F32),
            pltpu.VMEM((nr, NC, nx, 2, TILE, MSG), BF16),
            pltpu.VMEM((nr, nx, 2, TILE, MSG), BF16),
            pltpu.VMEM((nr, nx, 2, TILE, MSG), BF16),
            pltpu.VMEM((nr, nx, 2, TILE, MSG), BF16),
            pltpu.VMEM((nr, 2, TILE, MSG), BF16),
            pltpu.VMEM((nz, nx, TILE, MSG), BF16),
            pltpu.VMEM((nh, ROWS_DEV, hidden.shape[1]), F32),
            pltpu.VMEM((nh, ROWS_DEV, hidden.shape[1]), F32),
            dma((nz, nx)), dma((nz, nx)), dma((nx,)), dma((nx,)), dma, dma,
            dma((nz,)), dma((nz,)), dma((nx,)), dma((nx,)), dma, dma,
            dma((nr,)), dma((nr,)), dma((nr, nx)), dma((nr, nx)), dma((nr, 2, nx)), dma((nz, nx)), dma((nh,)), dma((nh,)),
            dma((nr, 2)), dma, dma((11,)),
        ],
        compiler_params=pltpu.CompilerParams(collective_id=0, has_side_effects=True, vmem_limit_bytes=48 << 20),
    )(*to_hbm)
    return pl.pallas_call(
        functools.partial(store_kernel, nr),
        out_shape=(
            jax.ShapeDtypeStruct(hidden.shape, BF16),
            jax.ShapeDtypeStruct(cache_k.shape, BF16),
            jax.ShapeDtypeStruct(cache_v.shape, BF16),
        ),
        in_specs=[vmem] * 3,
        out_specs=(hbm, hbm, hbm),
        scratch_shapes=[dma((2 * nr + 1,))],
        compiler_params=pltpu.CompilerParams(vmem_limit_bytes=2 << 20),
    )(*[pltpu.with_memory_space_constraint(a, pltpu.MemorySpace.VMEM) for a in (mixed, kc, vc)])


def build(mesh, nz, nx, window):
    seq_rows = P("seq", "head")
    cache = P(None, "head", "seq", None)
    in_specs = (seq_rows,) * 4 + (cache, cache, P("head"), P(), P("head", None)) + (P(),) * 5
    return jax.shard_map(
        functools.partial(body, nz, nx, mesh.shape["head"], window),
        mesh=mesh,
        in_specs=in_specs,
        out_specs=(seq_rows, cache, cache),
        check_vma=False,
    )


def solution(mesh):
    return build(mesh, 8, 4, 4096)
```

```python
import functools
import math

import jax
import jax.numpy as jnp
from jax import lax
from jax.experimental import pallas as pl
from jax.experimental.pallas import tpu as pltpu
from jax.sharding import PartitionSpec as P

MESH = pl.DeviceIdType.MESH
F32 = jnp.float32
BF16 = jnp.bfloat16
I32 = jnp.int32

SINKS = 4
FILL_LOW = -1e30
EPSILON = 1e-05
OUT_SCALE = 0.8
LOG2E = 1.4426950408889634

STAGED = (0, 1)
NC = 2
ROWS_DEV = 4
CHUNKS = 4
TILE = ROWS_DEV * CHUNKS
QK = 128
VD = 256
MSG = VD + 128


def nt(a, b):
    return lax.dot_general(a, b, (((1,), (1,)), ((), ())), preferred_element_type=F32)


def iota(shape, dim):
    return lax.broadcasted_iota(I32, shape, dim)


def slot_of(index, nx):
    row = index % ROWS_DEV
    zl = (index // TILE) % 2
    x = (index // (2 * TILE)) % nx
    core = index // (2 * TILE * nx)
    return ((zl * nx + x) * NC + core) * ROWS_DEV + row


def chunk_of(index):
    return (index // ROWS_DEV) % CHUNKS


def tile_of(ref):
    value = ref[...].astype(F32)
    pieces = [value[:, QK * c : QK * (c + 1)] for c in range(CHUNKS)]
    return jnp.concatenate(pieces, axis=0).astype(BF16)


def unpack(message):
    wide = message.astype(F32)
    shift = wide[:, VD : VD + 1]
    total = wide[:, VD + 1 : VD + 2] + wide[:, VD + 2 : VD + 3]
    return shift, total, wide[:, :VD]


def merge(parts):
    peak = functools.reduce(jnp.maximum, [p[0] for p in parts])
    factors = [jnp.exp2(p[0] - peak) for p in parts]
    total = sum(f * p[1] for f, p in zip(factors, parts))
    weighted = sum(f * p[2] for f, p in zip(factors, parts))
    return peak, total, weighted


def stat_lanes(shift, total):
    high = total.astype(BF16).astype(F32)
    lane = iota((shift.shape[0], 128), 1)
    return jnp.where(lane == 0, shift, jnp.where(lane == 1, high, total - high))


def pack(part):
    shift, total, weighted = part
    return weighted.astype(BF16), stat_lanes(shift, total).astype(BF16)


def attention_kernel(
    nz, nx, nh, window,
    lengths_in, draft_counts_in, lambdas_in, hidden_in, queries_in, keys_in, values_in, gain_in, parents_in,
    path_in, accepted_in, cache_k, cache_v, out_weight,
    mixed, kc, vc,
    path, accepted, lengths, draft_counts, lambdas, hidden, queries, keys, values, gain, parents,
    gq, gkv, wv, tree, oldest, part, core_in, chip, x_in, plane, z_in, y_out, y_in,
    qz_s, qz_r, qx_s, qx_r, qc_s, qc_r, kz_s, kz_r, kx_s, kx_r, kc_s, kc_r,
    rc_s, rc_r, rx_s, rx_r, rz_s, rz_r, y_s, y_r, load_sem, w_sem, small_sem,
):
    nr = nz // 2
    slots = 2 * nx * NC * ROWS_DEV
    span = cache_k.shape[2]
    rows = 2 * nx * NC * TILE
    head_rows = rows // 2
    seq = lax.axis_index("seq")
    head = lax.axis_index("head")
    core = seq % NC
    x = (seq // NC) % nx
    z = seq // (NC * nx)

    def device(zz, xx, cc):
        return ((zz * nx + xx) * NC + cc, head)

    def remote(src, dst, send, recv, target):
        return pltpu.make_async_remote_copy(
            src_ref=src, dst_ref=dst, send_sem=send, recv_sem=recv, device_id=target, device_id_type=MESH
        )

    z_peers = [(d, (z + d) % nz, (z + nz - d) % nz) for d in range(1, nz)]
    x_peers = [(d, (x + d) % nx, (x + nx - d) % nx) for d in range(1, nx)]
    h_peers = [(d, (head + d) % nh, (head + nh - d) % nh) for d in range(1, nh)]
    other = 1 - core
    own = z // 2
    even = 1 - z % 2
    order = [(own + nr // 2) % nr, (own + nr - 1 + 2 * even) % nr, (own + nr + 1 - 2 * even) % nr, own]
    last = len(order) - 1

    small = [
        pltpu.make_async_copy(src, dst, small_sem.at[i])
        for i, (src, dst) in enumerate(
            [
                (queries_in, queries), (keys_in, keys), (values_in, values), (parents_in, parents), (lengths_in, lengths),
                (path_in, path), (accepted_in, accepted), (draft_counts_in, draft_counts), (lambdas_in, lambdas), (hidden_in, hidden), (gain_in, gain),
            ]
        )
    ]
    small[0].start()
    barrier = pltpu.get_barrier_semaphore()
    peers = [device(z, x, other)]
    peers += [device(to, x, core) for _, to, _ in z_peers]
    peers += [device(z, to, core) for _, to, _ in x_peers]
    peers += [device((z + dz) % nz, (x + dx) % nx, core) for dz in range(1, nz) for dx in range(1, nx)]
    peers += [(seq, to) for _, to, _ in h_peers]
    for peer in peers:
        pl.semaphore_signal(barrier, inc=1, device_id=peer, device_id_type=MESH)

    loads = []
    for r in range(nr):
        loads.append(
            (
                pltpu.make_async_copy(cache_k.at[r], kc.at[r], load_sem.at[r, 0]),
                pltpu.make_async_copy(cache_v.at[r], vc.at[r], load_sem.at[r, 1]),
            )
        )
    load_w = pltpu.make_async_copy(out_weight, wv, w_sem)
    for copy in small[1:]:
        copy.start()
    small[0].wait()
    gq[core, x, z] = tile_of(queries)

    pl.semaphore_wait(barrier, len(peers))

    sent = []

    def gather_z(buf, send, recv):
        waits = []
        for d, to, source in z_peers:
            copy = remote(buf.at[core, x, z], buf.at[core, x, z], send.at[d], recv.at[d], device(to, x, core))
            copy.start()
            sent.append(copy)
            waits.append(remote(buf.at[core, x, z], buf.at[core, x, source], send.at[d], recv.at[d], device(to, x, core)))
        return waits

    def gather_x(buf, send, recv):
        waits = []
        for d, to, source in x_peers:
            copy = remote(buf.at[core, x], buf.at[core, x], send.at[d], recv.at[d], device(z, to, core))
            copy.start()
            sent.append(copy)
            waits.append(remote(buf.at[core, x], buf.at[core, source], send.at[d], recv.at[d], device(z, to, core)))
        return waits

    def gather_core(buf, send, recv):
        copy = remote(buf.at[core], buf.at[core], send, recv, device(z, x, other))
        copy.start()
        sent.append(copy)
        return [remote(buf.at[core], buf.at[other], send, recv, device(z, x, other))]

    def arrived(waits):
        for copy in waits:
            copy.wait_recv()

    q_all = []
    for dz in sorted(range(nz), key=lambda i: -min(i, nz - i)):
        for dx in sorted(range(nx), key=lambda i: -min(i, nx - i)):
            if dz + dx > 0:
                mine = gq.at[core, x, z]
                target = device((z + dz) % nz, (x + dx) % nx, core)
                copy = remote(mine, mine, qz_s.at[dz, dx], qz_r.at[dz, dx], target)
                copy.start()
                sent.append(copy)
                theirs = gq.at[core, (x + nx - dx) % nx, (z + nz - dz) % nz]
                q_all.append(remote(mine, theirs, qz_s.at[dz, dx], qz_r.at[dz, dx], target))
    for copy_k, copy_v in loads:
        copy_k.start()
        copy_v.start()
    load_w.start()
    for copy in small[1:]:
        copy.wait()
    gkv[core, x, z, 0] = tile_of(keys)
    gkv[core, x, z, 1] = tile_of(values)
    kv_z = gather_z(gkv, kz_s, kz_r)

    line = iota((head_rows, slots), 0)
    row_slot = slot_of(line // (2 * ROWS_DEV) * TILE + line % ROWS_DEV, nx)
    row_pick = (row_slot == iota((head_rows, slots), 1)).astype(BF16)
    first_map = (iota((head_rows, 1), 0) // ROWS_DEV) % 2 == 0
    low = iota((slots, slots), 0)
    high = iota((slots, slots), 1)
    trees = []
    for r in range(nr):
        link = (low == parents[r : r + 1, :]) & (high >= 1)
        trees.append((link | (low == high)).astype(F32).astype(BF16))
    for _ in range(max(1, (slots - 1).bit_length())):
        trees = [jnp.minimum(jnp.dot(t, t, preferred_element_type=F32), 1.0).astype(BF16) for t in trees]
    for r in range(nr):
        tree[r] = trees[r]
        depth = jnp.sum(nt(row_pick, trees[r]), axis=1, keepdims=True) - 1.0
        oldest[r] = depth + (lengths[r] - window).astype(F32)

    arrived(q_all)
    q_c = gather_core(gq, qc_s, qc_r)
    arrived(kv_z)
    kv_x = gather_x(gkv, kx_s, kx_r)
    arrived(q_c)

    scale = LOG2E / math.sqrt(QK)
    position = (seq * span + iota((1, span), 1)).astype(F32)

    def attend(k):
        r = order[k]
        q = gq[:, :, pl.ds(2 * r, 2)].reshape(rows, QK).astype(F32).reshape(rows // TILE, 2, 2 * ROWS_DEV, QK)
        reach = jnp.where(position < SINKS, -FILL_LOW, position)
        reach = jnp.where(position < lengths[r].astype(F32), reach, FILL_LOW)
        allowed = reach > oldest[r]
        bodies, stats = [], []
        for h in range(2):
            mine = q[:, h].reshape(head_rows, QK)
            wide = jnp.concatenate([jnp.where(first_map, mine, 0.0), jnp.where(first_map, 0.0, mine)], axis=1).astype(BF16)
            scores = jnp.where(allowed, nt(wide, kc[r, h]) * scale, FILL_LOW)
            shift = jnp.max(scores, axis=1, keepdims=True).astype(BF16).astype(F32)
            weight = jnp.where(allowed, jnp.exp2(scores - shift), 0.0)
            total = jnp.sum(weight, axis=1, keepdims=True)
            bodies.append(jnp.dot(weight.astype(BF16), vc[r, h], preferred_element_type=F32))
            stats.append(stat_lanes(shift, total))

        def weave(pair):
            width = pair[0].shape[1]
            pair = [p.reshape(rows // TILE, 1, 2 * ROWS_DEV, width) for p in pair]
            return jnp.concatenate(pair, axis=1).reshape(rows, width).astype(BF16).reshape(NC, nx, 2, TILE, width)

        part[k, :, :, :, :, :VD] = weave(bodies)
        part[k, :, :, :, :, VD:] = weave(stats)
        copy = remote(part.at[k, other], core_in.at[k], rc_s.at[k], rc_r.at[k], device(z, x, other))
        copy.start()
        sent.append(copy)
        return copy

    def chip_merge(k, copy):
        copy.wait_recv()
        block = nx * 2 * TILE
        mine = part[k, core].reshape(block, MSG)
        theirs = core_in[k].reshape(block, MSG)
        body, stats = pack(merge([unpack(mine), unpack(theirs)]))
        chip[k, :, :, :, :VD] = body.reshape(nx, 2, TILE, VD)
        chip[k, :, :, :, VD:] = stats.reshape(nx, 2, TILE, 128)

    def send_x(k):
        waits = []
        for d, to, source in x_peers:
            copy = remote(chip.at[k, to], x_in.at[k, d], rx_s.at[k, d], rx_r.at[k, d], device(z, to, core))
            copy.start()
            sent.append(copy)
            waits.append(copy)
        return waits

    def to_owner(src, k, zl, d, zz, xx):
        copy = remote(src, z_in.at[z, x], rz_s.at[k, zl, d], rz_r.at[z, x], device(zz, xx, core))
        copy.start()
        sent.append(copy)

    def plane_merge(k, waits):
        arrived(waits)
        parts = [unpack(chip[k, x].reshape(2 * TILE, MSG))]
        for d, _, _ in x_peers:
            parts.append(unpack(x_in[k, d].reshape(2 * TILE, MSG)))
        body, stats = pack(merge(parts))
        plane[k, :, :, :VD] = body.reshape(2, TILE, VD)
        plane[k, :, :, VD:] = stats.reshape(2, TILE, 128)
        if k == last:
            to_owner(plane.at[k, 1 - z % 2], k, 0, 0, z + 2 * even - 1, x)
            z_in[z, x] = plane[k, z % 2]
            return
        for zl in range(2):
            to_owner(plane.at[k, zl], k, zl, 0, 2 * order[k] + zl, x)

    def send_direct(k):
        if k < last:
            for d in range(nx - 1, -1, -1):
                for zl in range(2):
                    xx = (x + d) % nx
                    to_owner(chip.at[k, xx, zl], k, zl, d, 2 * order[k] + zl, xx)
            return
        mate = z + 2 * even - 1
        for d in range(nx - 1, -1, -1):
            xx = (x + d) % nx
            to_owner(chip.at[k, xx, mate % 2], k, 0, d, mate, xx)
            if d > 0:
                to_owner(chip.at[k, xx, z % 2], k, 1, d, z, xx)
        z_in[z, x] = chip[k, x, z % 2]

    for pair in loads:
        for copy in pair:
            copy.wait()
    in_core, in_x = {}, {}

    def spread(k):
        chip_merge(k, in_core[k])
        if k in STAGED:
            in_x[k] = send_x(k)
        else:
            send_direct(k)

    def settle(k):
        if k in STAGED:
            plane_merge(k, in_x[k])

    in_core[0] = attend(0)
    in_core[1] = attend(1)
    spread(0)
    in_core[2] = attend(2)
    spread(1)
    in_core[3] = attend(3)
    spread(2)
    arrived(kv_x)
    kv_c = gather_core(gkv, kc_s, kc_r)
    settle(0)
    spread(3)
    settle(1)
    settle(2)
    arrived(kv_c)
    row_chunk_lane = chunk_of(iota((slots, rows), 1))
    slot_lane = slot_of(iota((slots, rows), 1), nx)

    def write(r):
        begin = lengths[r] - seq * span
        taken = (iota((span, slots), 0) - begin == iota((span, slots), 1)) & (iota((span, slots), 1) < accepted[r])
        taken = taken.astype(BF16)
        place = iota((span, 1), 0) - begin
        touched = (place >= 0) & (place < accepted[r])
        slot_order = (path[r : r + 1, :] == iota((slots, slots), 0)).astype(BF16)
        lanes = (slot_lane == iota((slots, rows), 0)).astype(BF16)
        wide = lax.dot_general(slot_order, lanes, (((0,), (0,)), ((), ())), preferred_element_type=F32)
        for i, buf in enumerate((kc, vc)):
            block = gkv[:, :, 2 * r : 2 * r + 2, i].reshape(rows, 128)
            for h in range(2):
                kept = [
                    jnp.dot(
                        jnp.where(row_chunk_lane == 2 * h + half, wide, 0.0).astype(BF16), block, preferred_element_type=F32
                    ).astype(BF16)
                    for half in range(2)
                ]
                fresh = jnp.dot(taken, jnp.concatenate(kept, axis=1), preferred_element_type=F32)
                buf[r, h] = jnp.where(touched, fresh, buf[r, h].astype(F32)).astype(BF16)


    for r in range(nr - 1):
        write(r)

    own_slot = ((z % 2) * nx + x) * NC + core
    own_slot = own_slot * ROWS_DEV
    keys_own = gkv[:, :, pl.ds(2 * own, 2), 0].reshape(rows, QK)
    values_own = gkv[:, :, pl.ds(2 * own, 2), 1].reshape(rows, QK)
    pick_row = (own_slot + iota((TILE, slots), 0) % ROWS_DEV == iota((TILE, slots), 1)).astype(BF16)
    live = (iota((TILE, slots), 1) < draft_counts[own]).astype(F32)
    seen = (nt(pick_row, tree[own]) * live).astype(BF16)
    pick_lane = (slot_of(iota((slots, rows), 1), nx) == iota((slots, rows), 0)).astype(BF16)
    lane_chunk = chunk_of(iota((TILE, rows), 1))
    row_chunk = iota((TILE, rows), 0) // ROWS_DEV
    allowed = (jnp.dot(seen, pick_lane, preferred_element_type=F32) > 0.5) & (lane_chunk == row_chunk)
    scores = jnp.where(allowed, nt(gq[core, x, z], keys_own) * scale, FILL_LOW)
    shift = jnp.max(scores, axis=1, keepdims=True)
    weight = jnp.where(allowed, jnp.exp2(scores - shift), 0.0)
    total = jnp.sum(weight, axis=1, keepdims=True)
    even_chunk = row_chunk % 2 == 0
    ahead = pltpu.roll(weight, ROWS_DEV, 1)
    behind = pltpu.roll(weight, rows - ROWS_DEV, 1)
    left = jnp.where(even_chunk, weight, behind).astype(BF16)
    right = jnp.where(even_chunk, ahead, weight).astype(BF16)
    weighted = jnp.concatenate(
        [
            jnp.dot(left, values_own, preferred_element_type=F32),
            jnp.dot(right, values_own, preferred_element_type=F32),
        ],
        axis=1,
    )
    draft = (shift, total, weighted)

    parts = [draft, unpack(z_in[z, x])]

    def take(zz, xx):
        remote(plane.at[0, 0], z_in.at[zz, xx], rz_s.at[0, 0, 0], rz_r.at[zz, xx], device(zz, xx, core)).wait_recv()
        parts.append(unpack(z_in[zz, xx]))

    for d in range(nx):
        if last not in STAGED:
            take(z + 2 * even - 1, (x + d) % nx)
            if d > 0:
                take(z, (x + d) % nx)
        elif d == 0:
            take(z + 2 * even - 1, x)
    parts = [merge(parts)]
    for step in range(2, nz):
        source = (2 * own + step) % nz
        rank = {nz // 2: 0, nz // 2 + 1: 0, nz // 2 - 1: 1, nz - 2: 1}.get(step, 2)
        if rank in STAGED:
            take(source, x)
        else:
            for xx in range(nx):
                take(source, xx)
    peak, total, weighted = merge(parts)
    attended = weighted / total
    row_live = own_slot + iota((ROWS_DEV, 1), 0) < draft_counts[own]
    normed = []
    for h in range(2):
        first = attended[2 * h * ROWS_DEV : (2 * h + 1) * ROWS_DEV]
        second = attended[(2 * h + 1) * ROWS_DEV : (2 * h + 2) * ROWS_DEV]
        difference = first - lambdas[h] * second
        square = jnp.mean(difference * difference, axis=1, keepdims=True)
        scaled = difference * lax.rsqrt(square + EPSILON) * gain[...] * OUT_SCALE
        normed.append(jnp.where(row_live, scaled, 0.0).astype(BF16))
    load_w.wait()
    product = jnp.dot(jnp.concatenate(normed, axis=1), wv[...], preferred_element_type=F32)
    width = mixed.shape[1]
    for h in range(nh):
        y_out[h] = product[:, h * width : (h + 1) * width]
    waits = []
    for d, to, source in h_peers:
        copy = remote(y_out.at[to], y_in.at[d], y_s.at[d], y_r.at[d], (seq, to))
        copy.start()
        sent.append(copy)
        waits.append(copy)
    for r in range(nr - 1, nr):
        write(r)
    for copy in sent[: -len(waits)] if waits else sent:
        copy.wait_send()
    summed = y_out[head]
    arrived(waits)
    for d, _, _ in h_peers:
        summed = summed + y_in[d]
    mixed[...] = (summed + hidden[...].astype(F32)).astype(BF16)

    for copy in waits:
        copy.wait_send()


def store_kernel(nr, mixed_in, kc, vc, mixed, new_k, new_v, sem):
    copies = []
    for r in range(nr):
        copies.append(pltpu.make_async_copy(kc.at[r], new_k.at[r], sem.at[2 * r]))
        copies.append(pltpu.make_async_copy(vc.at[r], new_v.at[r], sem.at[2 * r + 1]))
    copies.append(pltpu.make_async_copy(mixed_in, mixed, sem.at[2 * nr]))
    for copy in copies:
        copy.start()
    for copy in copies:
        copy.wait()


def body(
    nz, nx, nh, window,
    hidden, draft_queries, draft_keys, draft_values, cache_k, cache_v, lambdas, norm_gain, out_weight,
    lengths, parents, draft_counts, accepted_path, accepted_count,
):
    nr = nz // 2
    slots = 2 * nx * NC * ROWS_DEV
    rows = 2 * nx * NC * TILE
    vmem = pl.BlockSpec(memory_space=pltpu.VMEM)
    hbm = pl.BlockSpec(memory_space=pltpu.MemorySpace.HBM)
    dma = pltpu.SemaphoreType.DMA
    kv_shape = (NC, nx, nz, 2, TILE, 128)
    to_hbm = [
        pltpu.with_memory_space_constraint(a, pltpu.MemorySpace.HBM)
        for a in (
            lengths, draft_counts, lambdas, hidden, draft_queries, draft_keys, draft_values,
            norm_gain.reshape(1, VD), parents, accepted_path, accepted_count, cache_k, cache_v, out_weight,
        )
    ]
    mixed, kc, vc = pl.pallas_call(
        functools.partial(attention_kernel, nz, nx, nh, window),
        out_shape=(pltpu.VMEM(hidden.shape, BF16), pltpu.VMEM(cache_k.shape, BF16), pltpu.VMEM(cache_v.shape, BF16)),
        in_specs=[hbm] * 14,
        out_specs=(vmem, vmem, vmem),
        scratch_shapes=[
            pltpu.VMEM(accepted_path.shape, I32),
            pltpu.SMEM(accepted_count.shape, I32),
            pltpu.SMEM(lengths.shape, I32),
            pltpu.SMEM(draft_counts.shape, I32),
            pltpu.SMEM(lambdas.shape, F32),
            pltpu.VMEM(hidden.shape, BF16),
            pltpu.VMEM(hidden.shape, BF16),
            pltpu.VMEM(hidden.shape, BF16),
            pltpu.VMEM(hidden.shape, BF16),
            pltpu.VMEM((1, VD), F32),
            pltpu.VMEM(parents.shape, I32),
            pltpu.VMEM((NC, nx, nz, TILE, 128), BF16),
            pltpu.VMEM(kv_shape, BF16),
            pltpu.VMEM(out_weight.shape, BF16),
            pltpu.VMEM((nr, slots, slots), BF16),
            pltpu.VMEM((nr, rows // 2, 1), F32),
            pltpu.VMEM((nr, NC, nx, 2, TILE, MSG), BF16),
            pltpu.VMEM((nr, nx, 2, TILE, MSG), BF16),
            pltpu.VMEM((nr, nx, 2, TILE, MSG), BF16),
            pltpu.VMEM((nr, nx, 2, TILE, MSG), BF16),
            pltpu.VMEM((nr, 2, TILE, MSG), BF16),
            pltpu.VMEM((nz, nx, TILE, MSG), BF16),
            pltpu.VMEM((nh, ROWS_DEV, hidden.shape[1]), F32),
            pltpu.VMEM((nh, ROWS_DEV, hidden.shape[1]), F32),
            dma((nz, nx)), dma((nz, nx)), dma((nx,)), dma((nx,)), dma, dma,
            dma((nz,)), dma((nz,)), dma((nx,)), dma((nx,)), dma, dma,
            dma((nr,)), dma((nr,)), dma((nr, nx)), dma((nr, nx)), dma((nr, 2, nx)), dma((nz, nx)), dma((nh,)), dma((nh,)),
            dma((nr, 2)), dma, dma((11,)),
        ],
        compiler_params=pltpu.CompilerParams(collective_id=0, has_side_effects=True, vmem_limit_bytes=48 << 20),
    )(*to_hbm)
    return pl.pallas_call(
        functools.partial(store_kernel, nr),
        out_shape=(
            jax.ShapeDtypeStruct(hidden.shape, BF16),
            jax.ShapeDtypeStruct(cache_k.shape, BF16),
            jax.ShapeDtypeStruct(cache_v.shape, BF16),
        ),
        in_specs=[vmem] * 3,
        out_specs=(hbm, hbm, hbm),
        scratch_shapes=[dma((2 * nr + 1,))],
        compiler_params=pltpu.CompilerParams(vmem_limit_bytes=2 << 20),
    )(*[pltpu.with_memory_space_constraint(a, pltpu.MemorySpace.VMEM) for a in (mixed, kc, vc)])


def build(mesh, nz, nx, window):
    seq_rows = P("seq", "head")
    cache = P(None, "head", "seq", None)
    in_specs = (seq_rows,) * 4 + (cache, cache, P("head"), P(), P("head", None)) + (P(),) * 5
    return jax.shard_map(
        functools.partial(body, nz, nx, mesh.shape["head"], window),
        mesh=mesh,
        in_specs=in_specs,
        out_specs=(seq_rows, cache, cache),
        check_vma=False,
    )


def solution(mesh):
    return build(mesh, 8, 4, 4096)
```
